32 devices in a mesh: row: 8 (over y, x, core), col: 4 (over z).
Axes of the slice: x: 2, y: 2, z: 4, core: 2. Of those that a mesh axis runs over, the one named last changes fastest.
Arguments:
- ancestor_inverse: float32 [6144, 6144], P('row', 'col'), may hold values from -6 to 6
- factor: float32 [6144, 2560], P('row', 'col'), may hold values from -0.078125 to 0.078125
- diag_inverse: float32 [640, 2560], P('row', 'col'), may hold values from -6 to 6
- widths: int32 [4], replicated, may hold values from 384 to 640
- member: int32 [4, 6144], P(None, 'row'), may hold values 0 or 1
Outputs:
- offdiag: float32 [6144, 2560], P('row', 'col')
- diag_blocks: float32 [640, 2560], P('row', 'col')
The draws below stay inside these ranges and needn't reach their ends.
All inputs are finite; a program needn't handle non-finite values. No bound on the sum of `member` on one device may be relied on, other than what follows from the above.
Results may differ from the reference program's by a relative error of at most 0.0001.
Values sent between devices are 32-bit elements; how exact they have to be, the bound alone decides.
A program may use at most 128 MiB of HBM per device.

```python
import jax
import jax.numpy as jnp
from jax import lax

W = 640
NODES = 4
ANC = 6144
COLS = 2560


def place_ends(result, stream_key, least, largest):
    spot = [jax.random.randint(jax.random.fold_in(stream_key, axis), (), 0, length) for axis, length in enumerate(result.shape)]
    widest = result.shape.index(max(result.shape))
    neighbour = spot[:widest] + [(spot[widest] + 1) % result.shape[widest]] + spot[widest + 1:]
    return result.at[tuple(spot)].set(least).at[tuple(neighbour)].set(largest)


def block_scale(stream_key, extent, pieces, least, largest):
    gain, own = 1.0, jax.random.fold_in(stream_key, 6)
    for axis_at, parts in pieces:
        draws = jnp.exp(jax.random.uniform(jax.random.fold_in(own, axis_at), (parts,), jnp.float32, least / len(pieces), largest / len(pieces)))
        gain = gain * jnp.repeat(draws, extent[axis_at] // parts).reshape([-1 if axis == axis_at else 1 for axis in range(len(extent))])
    return gain


def noise(rng, shape, scale, reach, split=(), kind=jnp.bfloat16):
    array = scale * jax.random.normal(rng, shape, jnp.float32)
    if split:
        array = array * block_scale(rng, shape, split, -0.22, 0.18)
    return jnp.clip(array, -reach, reach).astype(kind)


def setup_inputs(seed: int = 0) -> dict:
    seeds = jax.random.split(jax.random.key(seed), 6)
    return {
        "ancestor_inverse": noise(seeds[0], (ANC, ANC), 1.0, 6.0, ((0, 8), (1, 4)), jnp.float32),
        "factor": noise(seeds[1], (ANC, COLS), ANC ** -0.5, 0.078125, ((0, 8), (1, 4)), jnp.float32),
        "diag_inverse": noise(seeds[2], (W, COLS), 1.0, 6.0, ((0, 8), (1, 4)), jnp.float32),
        "widths": place_ends(jax.random.randint(seeds[3], (NODES,), W * 3 // 5, W + 1), jax.random.fold_in(seeds[3], 1), W * 3 // 5, W).astype(jnp.int32),
        "member": place_ends((jax.random.randint(seeds[4], (NODES, ANC), 0, 4) < 3).astype(jnp.int32), jax.random.fold_in(seeds[4], 1), 0, 1),
    }


def reference(ancestor_inverse, factor, diag_inverse, widths, member):
    columns = jnp.arange(NODES * W, dtype=jnp.int32)
    node_of = columns // W
    within = columns % W
    width_col = widths[node_of]
    col_keep = (within < width_col).astype(jnp.float32)
    row_keep = member[node_of].T.astype(jnp.float32)
    mask = row_keep * col_keep[None, :]
    lexp = factor * mask
    product = jnp.dot(ancestor_inverse, lexp, precision=lax.Precision.HIGHEST, preferred_element_type=jnp.float32)
    offdiag = -product * mask
    blocks = []
    for node in range(NODES):
        left = lexp[:, node * W:(node + 1) * W]
        right = product[:, node * W:(node + 1) * W]
        blocks.append(jnp.dot(left.T, right, precision=lax.Precision.HIGHEST, preferred_element_type=jnp.float32))
    gram = jnp.concatenate(blocks, axis=1)
    inside = jnp.arange(W, dtype=jnp.int32)[:, None] < width_col[None, :]
    keep = inside.astype(jnp.float32) * col_keep[None, :]
    diag_blocks = (diag_inverse + gram) * keep
    return offdiag, diag_blocks
```

```python
import functools

import jax
import jax.numpy as jnp
from jax import lax
from jax.experimental import pallas as pl
from jax.experimental.pallas import tpu as pltpu
from jax.sharding import PartitionSpec as P

W = 640
NODES = 4
MESH = pl.DeviceIdType.MESH


def split(x):
    hi = x.astype(jnp.bfloat16)
    lo = (x - hi.astype(jnp.float32)).astype(jnp.bfloat16)
    return hi, lo


def row_tile(rows, most):
    return max(t for t in range(16, most + 1, 16) if rows % t == 0)


def product_kernel(
    R, C, a_ref, l_ref, left_ref, out_ref, gram_ref, mid, gath, part, recv, gram, inbox,
    a_hi, a_lo, b_hi, b_lo, s0, r0, s1, r1, s2, r2, s3, r3, s4, r4, s5, r5, own_sem,
):
    G = R // C
    half_ring = C // 2
    row = lax.axis_index("row")
    c = lax.axis_index("col")
    j = row // G
    g = lax.rem(row, G)
    rows, cols = l_ref.shape
    depth = a_ref.shape[1]
    chunk = rows // C
    half = rows // 2

    barrier = pltpu.get_barrier_semaphore()

    def greet(r, q):
        pl.semaphore_signal(barrier, inc=1, device_id=(r, q), device_id_type=MESH)

    for m in range(1, R):
        greet(lax.rem(row + m, R), c)
    for m in range(1, C):
        greet(row, lax.rem(c + m, C))
    pl.semaphore_wait(barrier, R + C - 2)

    def remote(src, dst, ssem, rsem, r, q):
        return pltpu.make_async_remote_copy(
            src_ref=src, dst_ref=dst, send_sem=ssem, recv_sem=rsem,
            device_id=(r, q), device_id_type=MESH,
        )

    mine = pl.ds(pl.multiple_of(j * chunk, chunk), chunk)

    def spread_copy(m):
        n = lax.rem(j + m, C)
        src = l_ref.at[pl.ds(pl.multiple_of(n * chunk, chunk), chunk)]
        return remote(src, mid.at[j], s0.at[m - 1], r0.at[m - 1], n * G + g, c)

    def column_copy(p, m):
        return remote(
            mid.at[p], gath.at[c, g, mine], s1.at[m - 1], r1.at[m - 1], row, p
        )

    for m in range(1, C):
        spread_copy(m).start()
    own = pltpu.make_async_copy(l_ref.at[mine], mid.at[j], own_sem.at[0])
    own.start()
    own.wait()
    for m in range(1, C):
        ref = mid.at[lax.rem(j + C - m, C)]
        remote(ref, ref, s0.at[m - 1], r0.at[m - 1], row, c).wait_recv()
    ways_on = sorted(range(1, C), key=lambda m: -min(m, C - m))
    for m in ways_on:
        column_copy(lax.rem(c + m, C), m).start()
    keep = pltpu.make_async_copy(mid.at[c], gath.at[c, g, mine], own_sem.at[1])
    keep.start()

    ta = row_tile(rows, 128)

    @pl.loop(0, rows // ta)
    def _(t):
        at = pl.ds(pl.multiple_of(t * ta, ta), ta)
        hi, lo = split(a_ref[at, :])
        a_hi[at, pl.ds(0, depth)] = hi
        a_lo[at, pl.ds(0, depth)] = lo

    order = [(0, 0), (half_ring, 0)]
    for s in range(half_ring - 1, 0, -1):
        order += [(s, -1), (s, 1)]
    blocks = []
    for s, way in order:
        blocks.append(lax.rem(c + (s if way >= 0 else C - s), C))

    def plane_copy(i, m):
        ref = gath.at[blocks[i], g, mine]
        return remote(ref, ref, s2.at[i, m - 1], r2.at[i, m - 1], lax.rem(j + m, C) * G + g, c)

    def plane_wait(i, m):
        from_j = lax.rem(j + C - m, C)
        ref = gath.at[blocks[i], g, pl.ds(pl.multiple_of(from_j * chunk, chunk), chunk)]
        remote(ref, ref, s2.at[i, m - 1], r2.at[i, m - 1], row, c).wait_recv()

    def group_copy(i, n):
        ref = gath.at[blocks[i], g]
        return remote(ref, ref, s3.at[i, n - 1], r3.at[i, n - 1], j * G + lax.rem(g + n, G), c)

    def group_wait(i, n):
        ref = gath.at[blocks[i], lax.rem(g + G - n, G)]
        remote(ref, ref, s3.at[i, n - 1], r3.at[i, n - 1], row, c).wait_recv()

    for i, (s, way) in enumerate(order):
        if s:
            m = C - s if way >= 0 else s
            ref = gath.at[blocks[i], g, mine]
            remote(ref, ref, s1.at[m - 1], r1.at[m - 1], row, c).wait_recv()
        else:
            keep.wait()
        for m in range(1, C):
            plane_copy(i, m).start()

    tb = row_tile(rows, 128)
    tm = row_tile(rows, 256)

    def multiply(i):
        q = blocks[i]
        for gg in range(G):
            @pl.loop(0, rows // tb)
            def _(t):
                hi, lo = split(gath[q, gg, pl.ds(pl.multiple_of(t * tb, tb), tb), :])
                at = pl.ds(pl.multiple_of(gg * rows + t * tb, tb), tb)
                b_hi[at, :] = hi
                b_lo[at, :] = lo

        @pl.loop(0, rows // tm)
        def _(t):
            at = pl.ds(pl.multiple_of(t * tm, tm), tm)
            dot = functools.partial(jnp.dot, preferred_element_type=jnp.float32)
            x_hi, x_lo = a_hi[at, pl.ds(0, depth)], a_lo[at, pl.ds(0, depth)]
            y_hi, y_lo = b_hi[pl.ds(0, depth), :], b_lo[pl.ds(0, depth), :]
            part[i, at, :] = dot(x_hi, y_lo) + dot(x_lo, y_hi) + dot(x_hi, y_hi)

    def ring_copy(i, way, s):
        to = lax.rem(c + (C - 1 if way == 0 else 1), C)
        piece = pl.ds(way * half, half) if s == half_ring else pl.ds(0, rows)
        return remote(
            part.at[i, piece], recv.at[way, s - 1, piece],
            s4.at[way, s - 1], r4.at[way, s - 1], row, to,
        )

    def ring_wait(way, s):
        piece = pl.ds(way * half, half) if s + 1 == half_ring else pl.ds(0, rows)
        ref = recv.at[way, s, piece]
        remote(ref, ref, s4.at[way, s], r4.at[way, s], row, c).wait_recv()

    def accumulate(i, way, s):
        lo, n = (way * half, half) if s + 1 == half_ring else (0, rows)
        step = row_tile(n, 128)

        @pl.loop(0, n // step)
        def _(t):
            at = pl.ds(pl.multiple_of(lo + t * step, 16), step)
            part[i, at, :] = part[i, at, :] + recv[way, s, at, :]

    sends = []
    for i, (s, way) in enumerate(order):
        for m in range(1, C):
            plane_wait(i, m)
        for n in range(1, G):
            group_copy(i, n).start()
        for n in range(1, G):
            group_wait(i, n)
        multiply(i)
        if s == half_ring:
            ways = (0, 1)
        elif s:
            ways = (0,) if way < 0 else (1,)
        else:
            ways = ()
        for w in ways:
            if s < half_ring:
                ring_wait(w, s)
                accumulate(i, w, s)
            copy = ring_copy(i, w, s)
            copy.start()
            sends.append(copy)

    ring_wait(0, 0)
    ring_wait(1, 0)

    @pl.loop(0, rows // ta)
    def _(t):
        at = pl.ds(pl.multiple_of(t * ta, ta), ta)
        x = part[0, at, :] + recv[0, 0, at, :] + recv[1, 0, at, :]
        out_ref[at, :] = x
        hi, lo = split(x)
        b_hi[at, :] = hi
        b_lo[at, :] = lo
        hi, lo = split(left_ref[at, :])
        a_hi[at, pl.ds(0, W)] = hi
        a_lo[at, pl.ds(0, W)] = lo

    for t in range(W // 128):
        at = pl.ds(t * 128, 128)
        dot = functools.partial(
            lax.dot_general, dimension_numbers=(((0,), (0,)), ((), ())),
            preferred_element_type=jnp.float32,
        )
        p_hi, p_lo = b_hi[pl.ds(0, rows), :], b_lo[pl.ds(0, rows), :]
        x = dot(a_hi[:, at], p_lo) + dot(a_lo[:, at], p_hi)
        gram[at, :] = x + dot(a_hi[:, at], p_hi)

    share = W // R

    def gram_copy(m):
        to = lax.rem(row + m, R)
        src = gram.at[pl.ds(pl.multiple_of(to * share, 8), share)]
        return remote(src, inbox.at[m - 1], s5.at[m - 1], r5.at[m - 1], to, c)

    for m in range(1, R):
        gram_copy(m).start()
    total = gram[pl.ds(pl.multiple_of(row * share, 8), share), :]
    for m in range(1, R):
        gram_copy(m).wait_recv()
        total = total + inbox[m - 1]
    gram_ref[...] = total

    for copy in sends:
        copy.wait_send()
    for m in range(1, C):
        spread_copy(m).wait_send()
        column_copy(lax.rem(c + m, C), m).wait_send()
    for m in range(1, R):
        gram_copy(m).wait_send()
    for i in range(C):
        for m in range(1, C):
            plane_copy(i, m).wait_send()
        for n in range(1, G):
            group_copy(i, n).wait_send()


def grid_product(R, C, a, l, left):
    rows, cols = l.shape
    G = R // C
    depth = a.shape[1]
    vmem = pl.BlockSpec(memory_space=pltpu.VMEM)
    dma = pltpu.SemaphoreType.DMA
    return pl.pallas_call(
        functools.partial(product_kernel, R, C),
        out_shape=[
            jax.ShapeDtypeStruct((rows, cols), jnp.float32),
            jax.ShapeDtypeStruct((W // R, cols), jnp.float32),
        ],
        in_specs=[vmem, vmem, vmem],
        out_specs=[vmem, vmem],
        scratch_shapes=[
            pltpu.VMEM((C, rows // C, cols), jnp.float32),
            pltpu.VMEM((C, G, rows, cols), jnp.float32),
            pltpu.VMEM((C, rows, cols), jnp.float32),
            pltpu.VMEM((2, C // 2, rows, cols), jnp.float32),
            pltpu.VMEM((W, cols), jnp.float32),
            pltpu.VMEM((R - 1, W // R, cols), jnp.float32),
            pltpu.VMEM((rows, max(depth, W)), jnp.bfloat16),
            pltpu.VMEM((rows, max(depth, W)), jnp.bfloat16),
            pltpu.VMEM((max(depth, rows), cols), jnp.bfloat16),
            pltpu.VMEM((max(depth, rows), cols), jnp.bfloat16),
            dma((C - 1,)),
            dma((C - 1,)),
            dma((C - 1,)),
            dma((C - 1,)),
            dma((C, C - 1)),
            dma((C, C - 1)),
            dma((C, max(G - 1, 1))),
            dma((C, max(G - 1, 1))),
            dma((2, C // 2)),
            dma((2, C // 2)),
            dma((R - 1,)),
            dma((R - 1,)),
            dma((2,)),
        ],
        compiler_params=pltpu.CompilerParams(
            collective_id=0, has_side_effects=True, vmem_limit_bytes=67043328
        ),
    )(a, l, left)


def pieces_of(tiles):
    out, at = [], 0
    while at < tiles:
        n = min(2, tiles - at)
        out.append((at, n))
        at += n
    return out


def line_kernel(
    R, C, a_hbm, f_hbm, diag_ref, widths_ref, member_ref, out_ref, dout_ref,
    a_raw, f_raw, mask, lm, gath, part, recv, a_hi, a_lo, b_hi, b_lo, t_hi, t_lo,
    gram, inbox, in_sem, own_sem, s0, r0, s1, r1, s2, r2, s3, r3, s4, r4, s5, r5,
):
    rows, depth = a_raw.shape
    tiles = lm.shape[0]
    G = R // C
    chunk = rows // C
    half = chunk // 2
    share = W // R
    pieces = pieces_of(tiles)
    row = lax.axis_index("row")
    c = lax.axis_index("col")
    j = row // G
    g = lax.rem(row, G)
    other = 1 - g
    jx = j + 1 - 2 * lax.rem(j, 2)
    jy = lax.rem(j + 2, C)
    jd = C - 1 - j
    last = C - 1
    h = c // 2
    m = c + h * (last - 2 * c)

    def flip(n):
        return n + h * (last - 2 * n)

    blocks = [flip(3), flip(2 - 2 * m), flip(1 + m), c]
    onward = [flip(m + 1), flip(1 - m), flip(m + 1)]
    slots = [blocks[0], blocks[1], blocks[2] + m * (C - blocks[2])]

    load_f = pltpu.make_async_copy(f_hbm, f_raw, in_sem.at[0])
    load_a = pltpu.make_async_copy(a_hbm, a_raw, in_sem.at[1])
    load_f.start()
    load_a.start()

    barrier = pltpu.get_barrier_semaphore()

    def greet(r, q):
        pl.semaphore_signal(barrier, inc=1, device_id=(r, q), device_id_type=MESH)

    for n in range(1, R):
        greet(lax.rem(row + n, R), c)

    @pl.when(c > 0)
    def _():
        greet(row, c - 1)

    @pl.when(c < last)
    def _():
        greet(row, c + 1)

    for q in range(C):
        @pl.when((j != c) | (c != q))
        def _():
            greet(c * G + g, q)

    keep = lax.broadcasted_iota(jnp.int32, (NODES, 128), 0) == c
    width = widths_ref[c]
    member = member_ref[...].astype(jnp.float32).astype(jnp.bfloat16)
    load_f.wait()
    for t in range(tiles):
        q = lax.broadcasted_iota(jnp.int32, (NODES, 128), 1) + t * 128
        pick = jnp.where(keep & (q < width), 1.0, 0.0).astype(jnp.bfloat16)
        x = lax.dot_general(
            member, pick, (((0,), (0,)), ((), ())), preferred_element_type=jnp.float32
        )
        mask[t] = x
        lm[t] = f_raw[:, t * 128:(t + 1) * 128] * x

    pl.semaphore_wait(barrier, R - 1 + C + m + (j != c).astype(jnp.int32))

    def remote(src, dst, ssem, rsem, r, q):
        return pltpu.make_async_remote_copy(
            src_ref=src, dst_ref=dst, send_sem=ssem, recv_sem=rsem,
            device_id=(r, q), device_id_type=MESH,
        )

    def at_tiles(p):
        t, n = pieces[p]
        return pl.ds(t, n)

    def spot(gg, jj, n=None, k=0):
        start = gg * rows + jj * chunk + k * half
        return pl.ds(pl.multiple_of(start, 8), half if n else chunk)

    def spread_copy(jj, p):
        src = lm.at[at_tiles(p), pl.ds(jj * chunk, chunk)]
        dst = gath.at[c, at_tiles(p), spot(g, jj)]
        return remote(src, dst, s0.at[jj, p], r0.at[c, p], jj * G + g, j)

    def own_copy(jj, p):
        src = lm.at[at_tiles(p), pl.ds(jj * chunk, chunk)]
        dst = gath.at[c, at_tiles(p), spot(g, jj)]
        return pltpu.make_async_copy(src, dst, own_sem.at[p])

    for p in range(len(pieces)):
        for jj in range(C):
            @pl.when((j != jj) | (c != jj))
            def _():
                spread_copy(jj, p).start()

            @pl.when((j == jj) & (c == jj))
            def _():
                own_copy(jj, p).start()

    load_a.wait()
    ta = row_tile(rows, 128)

    @pl.loop(0, rows // ta)
    def _(t):
        at = pl.ds(pl.multiple_of(t * ta, ta), ta)
        hi, lo = split(a_raw[at, :])
        a_hi[at, :] = hi
        a_lo[at, :] = lo

    for t in range(tiles):
        hi, lo = split(lm[t].T)
        t_hi[pl.ds(t * 128, 128), :] = hi
        t_lo[pl.ds(t * 128, 128), :] = lo

    units = [(i, p) for p in range(len(pieces)) for i in range(C)]

    def take(u):
        i, p = units[u]
        q = blocks[i]
        ref = gath.at[q, at_tiles(p), spot(g, j)]
        return remote(ref, ref, s0.at[0, p], r0.at[q, p], row, c)

    def pass_copy(u, way):
        i, p = units[u]
        ref = gath.at[blocks[i], at_tiles(p), spot(g, j)]
        to = jx if way == 0 else jy
        return remote(ref, ref, s1.at[u, way], r1.at[u, way], to * G + g, c)

    def pass_wait(u, way):
        i, p = units[u]
        ref = gath.at[blocks[i], at_tiles(p), spot(g, jx if way == 0 else jy)]
        remote(ref, ref, s1.at[u, way], r1.at[u, way], row, c).wait_recv()

    def forward_copy(u, way):
        i, p = units[u]
        ref = gath.at[blocks[i], at_tiles(p), spot(g, jx if way == 0 else jy, 1, way)]
        to = jy if way == 0 else jx
        return remote(ref, ref, s2.at[u, way], r2.at[u, way], to * G + g, c)

    def forward_wait(u, way):
        i, p = units[u]
        ref = gath.at[blocks[i], at_tiles(p), spot(g, jd, 1, way)]
        remote(ref, ref, s2.at[u, way], r2.at[u, way], row, c).wait_recv()

    def swap_copy(u):
        i, p = units[u]
        ref = gath.at[blocks[i], at_tiles(p), pl.ds(pl.multiple_of(g * rows, 8), rows)]
        return remote(ref, ref, s3.at[u], r3.at[u], j * G + other, c)

    def swap_wait(u):
        i, p = units[u]
        ref = gath.at[blocks[i], at_tiles(p), pl.ds(pl.multiple_of(other * rows, 8), rows)]
        remote(ref, ref, s3.at[u], r3.at[u], row, c).wait_recv()

    def sum_copy(u):
        i, p = units[u]
        return remote(
            part.at[i, at_tiles(p)], recv.at[slots[i], at_tiles(p)],
            s4.at[i, p], r4.at[slots[i], p], row, onward[i],
        )

    def sum_wait(slot, p):
        ref = recv.at[slot, at_tiles(p)]
        remote(ref, ref, s4.at[0, p], r4.at[slot, p], row, c).wait_recv()

    def stage_a(u):
        i, p = units[u]
        if i < C - 1:
            take(u).wait_recv()
        else:
            @pl.when(j != c)
            def _():
                take(u).wait_recv()

            @pl.when(j == c)
            def _():
                own_copy(0, p).wait()
        for way in range(2):
            pass_copy(u, way).start()

    def stage_b(u):
        for way in range(2):
            pass_wait(u, way)
            forward_copy(u, way).start()

    def stage_c(u):
        for way in range(2):
            forward_wait(u, way)
        swap_copy(u).start()

    tb = row_tile(depth, 256)
    tm = row_tile(rows, 384)

    def stage_d(u):
        i, p = units[u]
        t0, n = pieces[p]
        q = blocks[i]
        cols = pl.ds(0, n * 128)
        swap_wait(u)

        @pl.loop(0, depth // tb)
        def _(t):
            at = pl.ds(pl.multiple_of(t * tb, tb), tb)
            for k in range(n):
                hi, lo = split(gath[q, t0 + k, at, :])
                b_hi[at, pl.ds(k * 128, 128)] = hi
                b_lo[at, pl.ds(k * 128, 128)] = lo

        @pl.loop(0, rows // tm)
        def _(t):
            at = pl.ds(pl.multiple_of(t * tm, tm), tm)
            dot = functools.partial(jnp.dot, preferred_element_type=jnp.float32)
            x = dot(a_hi[at, :], b_lo[:, cols]) + dot(a_lo[at, :], b_hi[:, cols])
            x = x + dot(a_hi[at, :], b_hi[:, cols])
            for k in range(n):
                part[i, t0 + k, at, :] = x[:, k * 128:(k + 1) * 128]

        if i < C - 1:
            @pl.when(m == 0)
            def _():
                sum_copy(u).start()

    def add_in(i, slot, p):
        t0, n = pieces[p]

        @pl.loop(0, rows // ta)
        def _(t):
            at = pl.ds(pl.multiple_of(t * ta, ta), ta)
            for k in range(n):
                part[i, t0 + k, at, :] = part[i, t0 + k, at, :] + recv[slot, t0 + k, at, :]

    def stage_e(u):
        i, p = units[u]

        @pl.when(m == 1)
        def _():
            sum_wait(blocks[i], p)
            add_in(i, blocks[i], p)
            sum_copy(u).start()

    def gram_copy(n, p):
        to = lax.rem(row + n, R)
        return remote(
            gram.at[at_tiles(p), to], inbox.at[n - 1, at_tiles(p)],
            s5.at[n - 1, p], r5.at[n - 1, p], to, c,
        )

    def stage_f(p):
        t0, n = pieces[p]
        cols = pl.ds(0, n * 128)

        @pl.when(m == 1)
        def _():
            sum_wait(C, p)
            add_in(C - 1, C, p)

        sum_wait(c, p)

        @pl.loop(0, rows // ta)
        def _(t):
            at = pl.ds(pl.multiple_of(t * ta, ta), ta)
            for k in range(n):
                x = part[C - 1, t0 + k, at, :] + recv[c, t0 + k, at, :]
                out_ref[at, pl.ds((t0 + k) * 128, 128)] = -x * mask[t0 + k, at, :]
                hi, lo = split(x)
                b_hi[at, pl.ds(k * 128, 128)] = hi
                b_lo[at, pl.ds(k * 128, 128)] = lo

        dot = functools.partial(jnp.dot, preferred_element_type=jnp.float32)
        p_hi, p_lo = b_hi[pl.ds(0, rows), cols], b_lo[pl.ds(0, rows), cols]
        for r in range(R):
            at = pl.ds(r * share, share)
            x = dot(t_hi[at, :], p_lo) + dot(t_lo[at, :], p_hi) + dot(t_hi[at, :], p_hi)
            for k in range(n):
                gram[t0 + k, r] = x[:, k * 128:(k + 1) * 128]
        for k in range(1, R):
            gram_copy(k, p).start()

    def stage_g(p):
        t0, n = pieces[p]
        for k in range(1, R):
            gram_copy(k, p).wait_recv()
        for k in range(n):
            t = t0 + k
            x = gram[t, row]
            for d in range(R - 1):
                x = x + inbox[d, t]
            at = pl.ds(t * 128, 128)
            r = lax.broadcasted_iota(jnp.int32, (share, 128), 0) + row * share
            q = lax.broadcasted_iota(jnp.int32, (share, 128), 1) + t * 128
            inside = (r < width) & (q < width)
            dout_ref[:, at] = jnp.where(inside, diag_ref[:, at] + x, 0.0)

    total = len(units)
    finished = 0
    for step in range(total + 6):
        if step < total:
            stage_a(step)
        if 0 <= step - 1 < total:
            stage_b(step - 1)
        if 0 <= step - 2 < total:
            stage_c(step - 2)
        if 0 <= step - 3 < total:
            stage_d(step - 3)
        u = step - 5
        if 0 <= u < total:
            i, p = units[u]
            if i < C - 1:
                stage_e(u)
            late = p == len(pieces) - 1
            if p > 0 and i == (0 if late else C - 2):
                stage_f(p - 1)
                finished = p
    for p in range(finished, len(pieces)):
        stage_f(p)
    for p in range(len(pieces)):
        stage_g(p)

    for p in range(len(pieces)):
        for jj in range(C):
            @pl.when((j != jj) | (c != jj))
            def _():
                spread_copy(jj, p).wait_send()
        for k in range(1, R):
            gram_copy(k, p).wait_send()
    for u in range(total):
        for way in range(2):
            pass_copy(u, way).wait_send()
            forward_copy(u, way).wait_send()
        swap_copy(u).wait_send()
        if units[u][0] < C - 1:
            sum_copy(u).wait_send()


def line_product(R, C, a, f, diag, widths, member):
    rows, depth = a.shape
    cols = f.shape[1]
    tiles = cols // 128
    pieces = len(pieces_of(tiles))
    units = C * pieces
    f32, bf16 = jnp.float32, jnp.bfloat16
    vmem = pl.BlockSpec(memory_space=pltpu.VMEM)
    smem = pl.BlockSpec(memory_space=pltpu.SMEM)
    hbm = pl.BlockSpec(memory_space=pl.ANY)
    dma = pltpu.SemaphoreType.DMA
    return pl.pallas_call(
        functools.partial(line_kernel, R, C),
        out_shape=[
            jax.ShapeDtypeStruct((rows, cols), f32),
            jax.ShapeDtypeStruct((W // R, cols), f32),
        ],
        in_specs=[hbm, hbm, vmem, smem, vmem],
        out_specs=[vmem, vmem],
        scratch_shapes=[
            pltpu.VMEM((rows, depth), f32),
            pltpu.VMEM((rows, cols), f32),
            pltpu.VMEM((tiles, rows, 128), f32),
            pltpu.VMEM((tiles, rows, 128), f32),
            pltpu.VMEM((C, tiles, depth, 128), f32),
            pltpu.VMEM((C, tiles, rows, 128), f32),
            pltpu.VMEM((C + 1, tiles, rows, 128), f32),
            pltpu.VMEM((rows, depth), bf16),
            pltpu.VMEM((rows, depth), bf16),
            pltpu.VMEM((depth, 256), bf16),
            pltpu.VMEM((depth, 256), bf16),
            pltpu.VMEM((W, rows), bf16),
            pltpu.VMEM((W, rows), bf16),
            pltpu.VMEM((tiles, R, W // R, 128), f32),
            pltpu.VMEM((R - 1, tiles, W // R, 128), f32),
            dma((2,)),
            dma((pieces,)),
            dma((C, pieces)),
            dma((C, pieces)),
            dma((units, 2)),
            dma((units, 2)),
            dma((units, 2)),
            dma((units, 2)),
            dma((units,)),
            dma((units,)),
            dma((C - 1, pieces)),
            dma((C + 1, pieces)),
            dma((R - 1, pieces)),
            dma((R - 1, pieces)),
        ],
        compiler_params=pltpu.CompilerParams(
            collective_id=1, has_side_effects=True, vmem_limit_bytes=67043328
        ),
    )(a, f, diag, widths, member)


def per_device(ancestor_inverse, factor, diag_inverse, widths, member):
    R = lax.axis_size("row")
    C = lax.axis_size("col")
    my_row = lax.axis_index("row")
    my_col = lax.axis_index("col")
    shard_cols = factor.shape[1]
    rows, depth = ancestor_inverse.shape
    if C == NODES and R == 2 * C and shard_cols == W and depth == 2 * rows:
        return tuple(line_product(R, C, ancestor_inverse, factor, diag_inverse, widths, member))
    col_start = my_col * shard_cols
    global_cols = col_start + jnp.arange(shard_cols, dtype=jnp.int32)
    node_of = global_cols // W
    within = global_cols % W
    select = node_of[None, :] == jnp.arange(NODES, dtype=jnp.int32)[:, None]
    width_col = jnp.sum(jnp.where(select, widths[:, None], 0), axis=0)
    col_keep = within < width_col
    pick = jnp.where(select & col_keep[None, :], 1.0, 0.0).astype(jnp.bfloat16)
    mask = lax.dot_general(
        member.astype(jnp.bfloat16), pick, (((0,), (0,)), ((), ())),
        preferred_element_type=jnp.float32,
    )
    masked = factor * mask
    if shard_cols == W:
        left = masked
    else:
        rows_full = lax.all_gather(masked, "col", axis=1, tiled=True)
        left = lax.dynamic_slice_in_dim(rows_full, col_start // W * W, W, 1)
    product, gram = grid_product(R, C, ancestor_inverse, masked, left)
    offdiag = -product * mask
    diag_rows = diag_inverse.shape[0]
    local_rows = my_row * diag_rows + jnp.arange(diag_rows, dtype=jnp.int32)
    inside = (local_rows[:, None] < width_col[None, :]) & col_keep[None, :]
    diag_blocks = (diag_inverse + gram) * inside.astype(jnp.float32)
    return (offdiag, diag_blocks)


def solution(mesh):
    in_specs = (P("row", "col"), P("row", "col"), P("row", "col"), P(), P(None, "row"))
    out_specs = (P("row", "col"), P("row", "col"))
    return jax.shard_map(
        per_device, mesh=mesh, in_specs=in_specs, out_specs=out_specs, check_vma=False
    )
```

```python
import functools

import jax
import jax.numpy as jnp
from jax import lax
from jax.experimental import pallas as pl
from jax.experimental.pallas import tpu as pltpu
from jax.sharding import PartitionSpec as P

W = 640
NODES = 4
MESH = pl.DeviceIdType.MESH


def split(x):
    hi = x.astype(jnp.bfloat16)
    lo = (x - hi.astype(jnp.float32)).astype(jnp.bfloat16)
    return hi, lo


def row_tile(rows, most):
    return max(t for t in range(16, most + 1, 16) if rows % t == 0)


def product_kernel(
    R, C, a_ref, l_ref, left_ref, out_ref, gram_ref, mid, gath, part, recv, gram, inbox,
    a_hi, a_lo, b_hi, b_lo, s0, r0, s1, r1, s2, r2, s3, r3, s4, r4, s5, r5, own_sem,
):
    G = R // C
    half_ring = C // 2
    row = lax.axis_index("row")
    c = lax.axis_index("col")
    j = row // G
    g = lax.rem(row, G)
    rows, cols = l_ref.shape
    depth = a_ref.shape[1]
    chunk = rows // C
    half = rows // 2

    barrier = pltpu.get_barrier_semaphore()

    def greet(r, q):
        pl.semaphore_signal(barrier, inc=1, device_id=(r, q), device_id_type=MESH)

    for m in range(1, R):
        greet(lax.rem(row + m, R), c)
    for m in range(1, C):
        greet(row, lax.rem(c + m, C))
    pl.semaphore_wait(barrier, R + C - 2)

    def remote(src, dst, ssem, rsem, r, q):
        return pltpu.make_async_remote_copy(
            src_ref=src, dst_ref=dst, send_sem=ssem, recv_sem=rsem,
            device_id=(r, q), device_id_type=MESH,
        )

    mine = pl.ds(pl.multiple_of(j * chunk, chunk), chunk)

    def spread_copy(m):
        n = lax.rem(j + m, C)
        src = l_ref.at[pl.ds(pl.multiple_of(n * chunk, chunk), chunk)]
        return remote(src, mid.at[j], s0.at[m - 1], r0.at[m - 1], n * G + g, c)

    def column_copy(p, m):
        return remote(
            mid.at[p], gath.at[c, g, mine], s1.at[m - 1], r1.at[m - 1], row, p
        )

    for m in range(1, C):
        spread_copy(m).start()
    own = pltpu.make_async_copy(l_ref.at[mine], mid.at[j], own_sem.at[0])
    own.start()
    own.wait()
    for m in range(1, C):
        ref = mid.at[lax.rem(j + C - m, C)]
        remote(ref, ref, s0.at[m - 1], r0.at[m - 1], row, c).wait_recv()
    ways_on = sorted(range(1, C), key=lambda m: -min(m, C - m))
    for m in ways_on:
        column_copy(lax.rem(c + m, C), m).start()
    keep = pltpu.make_async_copy(mid.at[c], gath.at[c, g, mine], own_sem.at[1])
    keep.start()

    ta = row_tile(rows, 128)

    @pl.loop(0, rows // ta)
    def _(t):
        at = pl.ds(pl.multiple_of(t * ta, ta), ta)
        hi, lo = split(a_ref[at, :])
        a_hi[at, pl.ds(0, depth)] = hi
        a_lo[at, pl.ds(0, depth)] = lo

    order = [(0, 0), (half_ring, 0)]
    for s in range(half_ring - 1, 0, -1):
        order += [(s, -1), (s, 1)]
    blocks = []
    for s, way in order:
        blocks.append(lax.rem(c + (s if way >= 0 else C - s), C))

    def plane_copy(i, m):
        ref = gath.at[blocks[i], g, mine]
        return remote(ref, ref, s2.at[i, m - 1], r2.at[i, m - 1], lax.rem(j + m, C) * G + g, c)

    def plane_wait(i, m):
        from_j = lax.rem(j + C - m, C)
        ref = gath.at[blocks[i], g, pl.ds(pl.multiple_of(from_j * chunk, chunk), chunk)]
        remote(ref, ref, s2.at[i, m - 1], r2.at[i, m - 1], row, c).wait_recv()

    def group_copy(i, n):
        ref = gath.at[blocks[i], g]
        return remote(ref, ref, s3.at[i, n - 1], r3.at[i, n - 1], j * G + lax.rem(g + n, G), c)

    def group_wait(i, n):
        ref = gath.at[blocks[i], lax.rem(g + G - n, G)]
        remote(ref, ref, s3.at[i, n - 1], r3.at[i, n - 1], row, c).wait_recv()

    for i, (s, way) in enumerate(order):
        if s:
            m = C - s if way >= 0 else s
            ref = gath.at[blocks[i], g, mine]
            remote(ref, ref, s1.at[m - 1], r1.at[m - 1], row, c).wait_recv()
        else:
            keep.wait()
        for m in range(1, C):
            plane_copy(i, m).start()

    tb = row_tile(rows, 128)
    tm = row_tile(rows, 256)

    def multiply(i):
        q = blocks[i]
        for gg in range(G):
            @pl.loop(0, rows // tb)
            def _(t):
                hi, lo = split(gath[q, gg, pl.ds(pl.multiple_of(t * tb, tb), tb), :])
                at = pl.ds(pl.multiple_of(gg * rows + t * tb, tb), tb)
                b_hi[at, :] = hi
                b_lo[at, :] = lo

        @pl.loop(0, rows // tm)
        def _(t):
            at = pl.ds(pl.multiple_of(t * tm, tm), tm)
            dot = functools.partial(jnp.dot, preferred_element_type=jnp.float32)
            x_hi, x_lo = a_hi[at, pl.ds(0, depth)], a_lo[at, pl.ds(0, depth)]
            y_hi, y_lo = b_hi[pl.ds(0, depth), :], b_lo[pl.ds(0, depth), :]
            part[i, at, :] = dot(x_hi, y_lo) + dot(x_lo, y_hi) + dot(x_hi, y_hi)

    def ring_copy(i, way, s):
        to = lax.rem(c + (C - 1 if way == 0 else 1), C)
        piece = pl.ds(way * half, half) if s == half_ring else pl.ds(0, rows)
        return remote(
            part.at[i, piece], recv.at[way, s - 1, piece],
            s4.at[way, s - 1], r4.at[way, s - 1], row, to,
        )

    def ring_wait(way, s):
        piece = pl.ds(way * half, half) if s + 1 == half_ring else pl.ds(0, rows)
        ref = recv.at[way, s, piece]
        remote(ref, ref, s4.at[way, s], r4.at[way, s], row, c).wait_recv()

    def accumulate(i, way, s):
        lo, n = (way * half, half) if s + 1 == half_ring else (0, rows)
        step = row_tile(n, 128)

        @pl.loop(0, n // step)
        def _(t):
            at = pl.ds(pl.multiple_of(lo + t * step, 16), step)
            part[i, at, :] = part[i, at, :] + recv[way, s, at, :]

    sends = []
    for i, (s, way) in enumerate(order):
        for m in range(1, C):
            plane_wait(i, m)
        for n in range(1, G):
            group_copy(i, n).start()
        for n in range(1, G):
            group_wait(i, n)
        multiply(i)
        if s == half_ring:
            ways = (0, 1)
        elif s:
            ways = (0,) if way < 0 else (1,)
        else:
            ways = ()
        for w in ways:
            if s < half_ring:
                ring_wait(w, s)
                accumulate(i, w, s)
            copy = ring_copy(i, w, s)
            copy.start()
            sends.append(copy)

    ring_wait(0, 0)
    ring_wait(1, 0)

    @pl.loop(0, rows // ta)
    def _(t):
        at = pl.ds(pl.multiple_of(t * ta, ta), ta)
        x = part[0, at, :] + recv[0, 0, at, :] + recv[1, 0, at, :]
        out_ref[at, :] = x
        hi, lo = split(x)
        b_hi[at, :] = hi
        b_lo[at, :] = lo
        hi, lo = split(left_ref[at, :])
        a_hi[at, pl.ds(0, W)] = hi
        a_lo[at, pl.ds(0, W)] = lo

    for t in range(W // 128):
        at = pl.ds(t * 128, 128)
        dot = functools.partial(
            lax.dot_general, dimension_numbers=(((0,), (0,)), ((), ())),
            preferred_element_type=jnp.float32,
        )
        p_hi, p_lo = b_hi[pl.ds(0, rows), :], b_lo[pl.ds(0, rows), :]
        x = dot(a_hi[:, at], p_lo) + dot(a_lo[:, at], p_hi)
        gram[at, :] = x + dot(a_hi[:, at], p_hi)

    share = W // R

    def gram_copy(m):
        to = lax.rem(row + m, R)
        src = gram.at[pl.ds(pl.multiple_of(to * share, 8), share)]
        return remote(src, inbox.at[m - 1], s5.at[m - 1], r5.at[m - 1], to, c)

    for m in range(1, R):
        gram_copy(m).start()
    total = gram[pl.ds(pl.multiple_of(row * share, 8), share), :]
    for m in range(1, R):
        gram_copy(m).wait_recv()
        total = total + inbox[m - 1]
    gram_ref[...] = total

    for copy in sends:
        copy.wait_send()
    for m in range(1, C):
        spread_copy(m).wait_send()
        column_copy(lax.rem(c + m, C), m).wait_send()
    for m in range(1, R):
        gram_copy(m).wait_send()
    for i in range(C):
        for m in range(1, C):
            plane_copy(i, m).wait_send()
        for n in range(1, G):
            group_copy(i, n).wait_send()


def grid_product(R, C, a, l, left):
    rows, cols = l.shape
    G = R // C
    depth = a.shape[1]
    vmem = pl.BlockSpec(memory_space=pltpu.VMEM)
    dma = pltpu.SemaphoreType.DMA
    return pl.pallas_call(
        functools.partial(product_kernel, R, C),
        out_shape=[
            jax.ShapeDtypeStruct((rows, cols), jnp.float32),
            jax.ShapeDtypeStruct((W // R, cols), jnp.float32),
        ],
        in_specs=[vmem, vmem, vmem],
        out_specs=[vmem, vmem],
        scratch_shapes=[
            pltpu.VMEM((C, rows // C, cols), jnp.float32),
            pltpu.VMEM((C, G, rows, cols), jnp.float32),
            pltpu.VMEM((C, rows, cols), jnp.float32),
            pltpu.VMEM((2, C // 2, rows, cols), jnp.float32),
            pltpu.VMEM((W, cols), jnp.float32),
            pltpu.VMEM((R - 1, W // R, cols), jnp.float32),
            pltpu.VMEM((rows, max(depth, W)), jnp.bfloat16),
            pltpu.VMEM((rows, max(depth, W)), jnp.bfloat16),
            pltpu.VMEM((max(depth, rows), cols), jnp.bfloat16),
            pltpu.VMEM((max(depth, rows), cols), jnp.bfloat16),
            dma((C - 1,)),
            dma((C - 1,)),
            dma((C - 1,)),
            dma((C - 1,)),
            dma((C, C - 1)),
            dma((C, C - 1)),
            dma((C, max(G - 1, 1))),
            dma((C, max(G - 1, 1))),
            dma((2, C // 2)),
            dma((2, C // 2)),
            dma((R - 1,)),
            dma((R - 1,)),
            dma((2,)),
        ],
        compiler_params=pltpu.CompilerParams(
            collective_id=0, has_side_effects=True, vmem_limit_bytes=67043328
        ),
    )(a, l, left)


def pieces_of(tiles):
    out, at = [], 0
    while at < tiles:
        n = min(2, tiles - at)
        out.append((at, n))
        at += n
    return out


def line_kernel(
    R, C, a_hbm, f_hbm, diag_ref, widths_ref, member_ref, out_ref, dout_ref,
    a_raw, f_raw, mask, lm, mid, gath, part, recv, a_hi, a_lo, b_hi, b_lo, t_hi, t_lo,
    gram, inbox, in_sem, own_sem, s0, r0, s1, r1, s2, r2, s3, r3, s4, r4, s5, r5, s6, r6,
):
    rows, depth = a_raw.shape
    tiles = lm.shape[0]
    G = R // C
    chunk = rows // C
    half = chunk // 2
    share = W // R
    pieces = pieces_of(tiles)
    row = lax.axis_index("row")
    c = lax.axis_index("col")
    j = row // G
    g = lax.rem(row, G)
    other = 1 - g
    jx = j + 1 - 2 * lax.rem(j, 2)
    jy = lax.rem(j + 2, C)
    jd = C - 1 - j
    last = C - 1
    h = c // 2
    m = c + h * (last - 2 * c)

    def flip(n):
        return n + h * (last - 2 * n)

    blocks = [flip(3), flip(2 - 2 * m), flip(1 + m), c]
    onward = [flip(m + 1), flip(1 - m), flip(m + 1)]
    slots = [blocks[0], blocks[1], blocks[2] + m * (C - blocks[2])]

    load_f = pltpu.make_async_copy(f_hbm, f_raw, in_sem.at[0])
    load_a = pltpu.make_async_copy(a_hbm, a_raw, in_sem.at[1])
    load_f.start()
    load_a.start()

    barrier = pltpu.get_barrier_semaphore()

    def greet(r, q):
        pl.semaphore_signal(barrier, inc=1, device_id=(r, q), device_id_type=MESH)

    for n in range(1, R):
        greet(lax.rem(row + n, R), c)

    for n in range(1, C):
        greet(row, lax.rem(c + n, C))

    keep = lax.broadcasted_iota(jnp.int32, (NODES, 128), 0) == c
    width = widths_ref[c]
    member = member_ref[...].astype(jnp.float32).astype(jnp.bfloat16)
    load_f.wait()
    for t in range(tiles):
        q = lax.broadcasted_iota(jnp.int32, (NODES, 128), 1) + t * 128
        pick = jnp.where(keep & (q < width), 1.0, 0.0).astype(jnp.bfloat16)
        x = lax.dot_general(
            member, pick, (((0,), (0,)), ((), ())), preferred_element_type=jnp.float32
        )
        mask[t] = x
        lm[t] = f_raw[:, t * 128:(t + 1) * 128] * x

    pl.semaphore_wait(barrier, R + C - 2)

    def remote(src, dst, ssem, rsem, r, q):
        return pltpu.make_async_remote_copy(
            src_ref=src, dst_ref=dst, send_sem=ssem, recv_sem=rsem,
            device_id=(r, q), device_id_type=MESH,
        )

    def at_tiles(p):
        t, n = pieces[p]
        return pl.ds(t, n)

    def spot(gg, jj, n=None, k=0):
        start = gg * rows + jj * chunk + k * half
        return pl.ds(pl.multiple_of(start, 8), half if n else chunk)

    mine = pl.ds(pl.multiple_of(j * chunk, 8), chunk)

    def spread_copy(n, p):
        to = lax.rem(j + n, C)
        src = lm.at[at_tiles(p), pl.ds(pl.multiple_of(to * chunk, 8), chunk)]
        return remote(
            src, mid.at[j, at_tiles(p)], s0.at[n - 1, p], r0.at[n - 1, p], to * G + g, c
        )

    def spread_wait(n, p):
        ref = mid.at[lax.rem(j + C - n, C), at_tiles(p)]
        remote(ref, ref, s0.at[n - 1, p], r0.at[n - 1, p], row, c).wait_recv()

    def stay_copy(p):
        return pltpu.make_async_copy(lm.at[at_tiles(p), mine], mid.at[j, at_tiles(p)], own_sem.at[0, p])

    def line_copy(i, p):
        return remote(
            mid.at[blocks[i], at_tiles(p)], gath.at[c, at_tiles(p), spot(g, j)],
            s6.at[i, p], r6.at[c, p], row, blocks[i],
        )

    def keep_copy(p):
        return pltpu.make_async_copy(
            mid.at[c, at_tiles(p)], gath.at[c, at_tiles(p), spot(g, j)], own_sem.at[1, p]
        )

    def spread_start(p):
        for n in range(1, C):
            spread_copy(n, p).start()
        stay_copy(p).start()

    def line_start(p):
        stay_copy(p).wait()
        for n in range(1, C):
            spread_wait(n, p)
        for i in range(C - 1):
            line_copy(i, p).start()
        keep_copy(p).start()

    def line_sent(p):
        for i in range(C - 1):
            line_copy(i, p).wait_send()

    spread_start(0)
    load_a.wait()
    ta = row_tile(rows, 128)

    @pl.loop(0, rows // ta)
    def _(t):
        at = pl.ds(pl.multiple_of(t * ta, ta), ta)
        hi, lo = split(a_raw[at, :])
        a_hi[at, :] = hi
        a_lo[at, :] = lo

    for t in range(tiles):
        hi, lo = split(lm[t].T)
        t_hi[pl.ds(t * 128, 128), :] = hi
        t_lo[pl.ds(t * 128, 128), :] = lo

    line_start(0)
    for p in range(1, len(pieces)):
        spread_start(p)

    units = [(i, p) for p in range(len(pieces)) for i in range(C)]

    def take(u):
        i, p = units[u]
        if i == C - 1:
            keep_copy(p).wait()
        else:
            ref = gath.at[blocks[i], at_tiles(p), spot(g, j)]
            remote(ref, ref, s6.at[i, p], r6.at[blocks[i], p], row, c).wait_recv()

    def pass_copy(u, way):
        i, p = units[u]
        ref = gath.at[blocks[i], at_tiles(p), spot(g, j)]
        to = jx if way == 0 else jy
        return remote(ref, ref, s1.at[u, way], r1.at[u, way], to * G + g, c)

    def pass_wait(u, way):
        i, p = units[u]
        ref = gath.at[blocks[i], at_tiles(p), spot(g, jx if way == 0 else jy)]
        remote(ref, ref, s1.at[u, way], r1.at[u, way], row, c).wait_recv()

    def forward_copy(u, way):
        i, p = units[u]
        ref = gath.at[blocks[i], at_tiles(p), spot(g, jx if way == 0 else jy, 1, way)]
        to = jy if way == 0 else jx
        return remote(ref, ref, s2.at[u, way], r2.at[u, way], to * G + g, c)

    def forward_wait(u, way):
        i, p = units[u]
        ref = gath.at[blocks[i], at_tiles(p), spot(g, jd, 1, way)]
        remote(ref, ref, s2.at[u, way], r2.at[u, way], row, c).wait_recv()

    def swap_copy(u):
        i, p = units[u]
        ref = gath.at[blocks[i], at_tiles(p), pl.ds(pl.multiple_of(g * rows, 8), rows)]
        return remote(ref, ref, s3.at[u], r3.at[u], j * G + other, c)

    def swap_wait(u):
        i, p = units[u]
        ref = gath.at[blocks[i], at_tiles(p), pl.ds(pl.multiple_of(other * rows, 8), rows)]
        remote(ref, ref, s3.at[u], r3.at[u], row, c).wait_recv()

    def sum_copy(u):
        i, p = units[u]
        return remote(
            part.at[i, at_tiles(p)], recv.at[slots[i], at_tiles(p)],
            s4.at[i, p], r4.at[slots[i], p], row, onward[i],
        )

    def sum_wait(slot, p):
        ref = recv.at[slot, at_tiles(p)]
        remote(ref, ref, s4.at[0, p], r4.at[slot, p], row, c).wait_recv()

    def stage_a(u):
        take(u)
        for way in range(2):
            pass_copy(u, way).start()

    def stage_b(u):
        for way in range(2):
            pass_wait(u, way)
            forward_copy(u, way).start()

    def stage_c(u):
        for way in range(2):
            forward_wait(u, way)
        swap_copy(u).start()

    tb = row_tile(depth, 256)
    tm = row_tile(rows, 384)

    def stage_d(u):
        i, p = units[u]
        t0, n = pieces[p]
        q = blocks[i]
        cols = pl.ds(0, n * 128)
        swap_wait(u)

        @pl.loop(0, depth // tb)
        def _(t):
            at = pl.ds(pl.multiple_of(t * tb, tb), tb)
            for k in range(n):
                hi, lo = split(gath[q, t0 + k, at, :])
                b_hi[at, pl.ds(k * 128, 128)] = hi
                b_lo[at, pl.ds(k * 128, 128)] = lo

        @pl.loop(0, rows // tm)
        def _(t):
            at = pl.ds(pl.multiple_of(t * tm, tm), tm)
            dot = functools.partial(jnp.dot, preferred_element_type=jnp.float32)
            x = dot(a_hi[at, :], b_lo[:, cols]) + dot(a_lo[at, :], b_hi[:, cols])
            x = x + dot(a_hi[at, :], b_hi[:, cols])
            for k in range(n):
                part[i, t0 + k, at, :] = x[:, k * 128:(k + 1) * 128]

    def add_in(i, slot, p):
        t0, n = pieces[p]

        @pl.loop(0, rows // ta)
        def _(t):
            at = pl.ds(pl.multiple_of(t * ta, ta), ta)
            for k in range(n):
                part[i, t0 + k, at, :] = part[i, t0 + k, at, :] + recv[slot, t0 + k, at, :]

    def stage_e(u):
        i, p = units[u]

        @pl.when(m == 1)
        def _():
            sum_wait(blocks[i], p)
            add_in(i, blocks[i], p)

        if len(in_flight) == 2:
            sum_copy(in_flight.pop(0)).wait_send()
        sum_copy(u).start()
        in_flight.append(u)

    def gram_copy(n, p):
        to = lax.rem(row + n, R)
        return remote(
            gram.at[at_tiles(p), to], inbox.at[n - 1, at_tiles(p)],
            s5.at[n - 1, p], r5.at[n - 1, p], to, c,
        )

    def stage_f(p):
        t0, n = pieces[p]
        cols = pl.ds(0, n * 128)

        @pl.when(m == 1)
        def _():
            sum_wait(C, p)
            add_in(C - 1, C, p)

        sum_wait(c, p)

        @pl.loop(0, rows // ta)
        def _(t):
            at = pl.ds(pl.multiple_of(t * ta, ta), ta)
            for k in range(n):
                x = part[C - 1, t0 + k, at, :] + recv[c, t0 + k, at, :]
                out_ref[at, pl.ds((t0 + k) * 128, 128)] = -x * mask[t0 + k, at, :]
                hi, lo = split(x)
                b_hi[at, pl.ds(k * 128, 128)] = hi
                b_lo[at, pl.ds(k * 128, 128)] = lo

        dot = functools.partial(jnp.dot, preferred_element_type=jnp.float32)
        p_hi, p_lo = b_hi[pl.ds(0, rows), cols], b_lo[pl.ds(0, rows), cols]
        for r in range(R):
            at = pl.ds(r * share, share)
            x = dot(t_hi[at, :], p_lo) + dot(t_lo[at, :], p_hi) + dot(t_hi[at, :], p_hi)
            for k in range(n):
                gram[t0 + k, r] = x[:, k * 128:(k + 1) * 128]
        for k in range(1, R):
            gram_copy(k, p).start()

    def stage_g(p):
        t0, n = pieces[p]
        for k in range(1, R):
            gram_copy(k, p).wait_recv()
        for k in range(n):
            t = t0 + k
            x = gram[t, row]
            for d in range(R - 1):
                x = x + inbox[d, t]
            at = pl.ds(t * 128, 128)
            r = lax.broadcasted_iota(jnp.int32, (share, 128), 0) + row * share
            q = lax.broadcasted_iota(jnp.int32, (share, 128), 1) + t * 128
            inside = (r < width) & (q < width)
            dout_ref[:, at] = jnp.where(inside, diag_ref[:, at] + x, 0.0)

    total = len(units)
    finished = 0
    in_flight = []
    for step in range(total + 6):
        if step < total:
            stage_a(step)
        if 0 <= step - 1 < total:
            stage_b(step - 1)
        if step % C == 1 and step // C + 1 < len(pieces):
            line_sent(step // C)
            line_start(step // C + 1)
        if 0 <= step - 2 < total:
            stage_c(step - 2)
        if 0 <= step - 3 < total:
            stage_d(step - 3)
        u = step - 5
        if 0 <= u < total:
            i, p = units[u]
            if i < C - 1:
                stage_e(u)
            late = p == len(pieces) - 1
            if p > 0 and i == (0 if late else C - 2):
                stage_f(p - 1)
                finished = p
    for p in range(finished, len(pieces)):
        stage_f(p)
    for p in range(len(pieces)):
        stage_g(p)

    line_sent(len(pieces) - 1)
    for p in range(len(pieces)):
        for n in range(1, C):
            spread_copy(n, p).wait_send()
        for k in range(1, R):
            gram_copy(k, p).wait_send()
    for u in range(total):
        for way in range(2):
            pass_copy(u, way).wait_send()
            forward_copy(u, way).wait_send()
        swap_copy(u).wait_send()
    for u in in_flight:
        sum_copy(u).wait_send()


def line_product(R, C, a, f, diag, widths, member):
    rows, depth = a.shape
    cols = f.shape[1]
    tiles = cols // 128
    pieces = len(pieces_of(tiles))
    units = C * pieces
    f32, bf16 = jnp.float32, jnp.bfloat16
    vmem = pl.BlockSpec(memory_space=pltpu.VMEM)
    smem = pl.BlockSpec(memory_space=pltpu.SMEM)
    hbm = pl.BlockSpec(memory_space=pl.ANY)
    dma = pltpu.SemaphoreType.DMA
    return pl.pallas_call(
        functools.partial(line_kernel, R, C),
        out_shape=[
            jax.ShapeDtypeStruct((rows, cols), f32),
            jax.ShapeDtypeStruct((W // R, cols), f32),
        ],
        in_specs=[hbm, hbm, vmem, smem, vmem],
        out_specs=[vmem, vmem],
        scratch_shapes=[
            pltpu.VMEM((rows, depth), f32),
            pltpu.VMEM((rows, cols), f32),
            pltpu.VMEM((tiles, rows, 128), f32),
            pltpu.VMEM((tiles, rows, 128), f32),
            pltpu.VMEM((C, tiles, rows // C, 128), f32),
            pltpu.VMEM((C, tiles, depth, 128), f32),
            pltpu.VMEM((C, tiles, rows, 128), f32),
            pltpu.VMEM((C + 1, tiles, rows, 128), f32),
            pltpu.VMEM((rows, depth), bf16),
            pltpu.VMEM((rows, depth), bf16),
            pltpu.VMEM((depth, 256), bf16),
            pltpu.VMEM((depth, 256), bf16),
            pltpu.VMEM((W, rows), bf16),
            pltpu.VMEM((W, rows), bf16),
            pltpu.VMEM((tiles, R, W // R, 128), f32),
            pltpu.VMEM((R - 1, tiles, W // R, 128), f32),
            dma((2,)),
            dma((2, pieces)),
            dma((C - 1, pieces)),
            dma((C - 1, pieces)),
            dma((units, 2)),
            dma((units, 2)),
            dma((units, 2)),
            dma((units, 2)),
            dma((units,)),
            dma((units,)),
            dma((C - 1, pieces)),
            dma((C + 1, pieces)),
            dma((R - 1, pieces)),
            dma((R - 1, pieces)),
            dma((C - 1, pieces)),
            dma((C, pieces)),
        ],
        compiler_params=pltpu.CompilerParams(
            collective_id=1, has_side_effects=True, vmem_limit_bytes=67043328
        ),
    )(a, f, diag, widths, member)


def per_device(ancestor_inverse, factor, diag_inverse, widths, member):
    R = lax.axis_size("row")
    C = lax.axis_size("col")
    my_row = lax.axis_index("row")
    my_col = lax.axis_index("col")
    shard_cols = factor.shape[1]
    rows, depth = ancestor_inverse.shape
    if C == NODES and R == 2 * C and shard_cols == W and depth == 2 * rows:
        return tuple(line_product(R, C, ancestor_inverse, factor, diag_inverse, widths, member))
    col_start = my_col * shard_cols
    global_cols = col_start + jnp.arange(shard_cols, dtype=jnp.int32)
    node_of = global_cols // W
    within = global_cols % W
    select = node_of[None, :] == jnp.arange(NODES, dtype=jnp.int32)[:, None]
    width_col = jnp.sum(jnp.where(select, widths[:, None], 0), axis=0)
    col_keep = within < width_col
    pick = jnp.where(select & col_keep[None, :], 1.0, 0.0).astype(jnp.bfloat16)
    mask = lax.dot_general(
        member.astype(jnp.bfloat16), pick, (((0,), (0,)), ((), ())),
        preferred_element_type=jnp.float32,
    )
    masked = factor * mask
    if shard_cols == W:
        left = masked
    else:
        rows_full = lax.all_gather(masked, "col", axis=1, tiled=True)
        left = lax.dynamic_slice_in_dim(rows_full, col_start // W * W, W, 1)
    product, gram = grid_product(R, C, ancestor_inverse, masked, left)
    offdiag = -product * mask
    diag_rows = diag_inverse.shape[0]
    local_rows = my_row * diag_rows + jnp.arange(diag_rows, dtype=jnp.int32)
    inside = (local_rows[:, None] < width_col[None, :]) & col_keep[None, :]
    diag_blocks = (diag_inverse + gram) * inside.astype(jnp.float32)
    return (offdiag, diag_blocks)


def solution(mesh):
    in_specs = (P("row", "col"), P("row", "col"), P("row", "col"), P(), P(None, "row"))
    out_specs = (P("row", "col"), P("row", "col"))
    return jax.shard_map(
        per_device, mesh=mesh, in_specs=in_specs, out_specs=out_specs, check_vma=False
    )
```

```python
import functools

import jax
import jax.numpy as jnp
from jax import lax
from jax.experimental import pallas as pl
from jax.experimental.pallas import tpu as pltpu
from jax.sharding import PartitionSpec as P

W = 640
NODES = 4
MESH = pl.DeviceIdType.MESH


def split(x):
    hi = x.astype(jnp.bfloat16)
    lo = (x - hi.astype(jnp.float32)).astype(jnp.bfloat16)
    return hi, lo


def row_tile(rows, most):
    return max(t for t in range(16, most + 1, 16) if rows % t == 0)


def product_kernel(
    R, C, a_ref, l_ref, left_ref, out_ref, gram_ref, mid, gath, part, recv, gram, inbox,
    a_hi, a_lo, b_hi, b_lo, s0, r0, s1, r1, s2, r2, s3, r3, s4, r4, s5, r5, own_sem,
):
    G = R // C
    half_ring = C // 2
    row = lax.axis_index("row")
    c = lax.axis_index("col")
    j = row // G
    g = lax.rem(row, G)
    rows, cols = l_ref.shape
    depth = a_ref.shape[1]
    chunk = rows // C
    half = rows // 2

    barrier = pltpu.get_barrier_semaphore()

    def greet(r, q):
        pl.semaphore_signal(barrier, inc=1, device_id=(r, q), device_id_type=MESH)

    for m in range(1, R):
        greet(lax.rem(row + m, R), c)
    for m in range(1, C):
        greet(row, lax.rem(c + m, C))
    pl.semaphore_wait(barrier, R + C - 2)

    def remote(src, dst, ssem, rsem, r, q):
        return pltpu.make_async_remote_copy(
            src_ref=src, dst_ref=dst, send_sem=ssem, recv_sem=rsem,
            device_id=(r, q), device_id_type=MESH,
        )

    mine = pl.ds(pl.multiple_of(j * chunk, chunk), chunk)

    def spread_copy(m):
        n = lax.rem(j + m, C)
        src = l_ref.at[pl.ds(pl.multiple_of(n * chunk, chunk), chunk)]
        return remote(src, mid.at[j], s0.at[m - 1], r0.at[m - 1], n * G + g, c)

    def column_copy(p, m):
        return remote(
            mid.at[p], gath.at[c, g, mine], s1.at[m - 1], r1.at[m - 1], row, p
        )

    for m in range(1, C):
        spread_copy(m).start()
    own = pltpu.make_async_copy(l_ref.at[mine], mid.at[j], own_sem.at[0])
    own.start()
    own.wait()
    for m in range(1, C):
        ref = mid.at[lax.rem(j + C - m, C)]
        remote(ref, ref, s0.at[m - 1], r0.at[m - 1], row, c).wait_recv()
    ways_on = sorted(range(1, C), key=lambda m: -min(m, C - m))
    for m in ways_on:
        column_copy(lax.rem(c + m, C), m).start()
    keep = pltpu.make_async_copy(mid.at[c], gath.at[c, g, mine], own_sem.at[1])
    keep.start()

    ta = row_tile(rows, 128)

    @pl.loop(0, rows // ta)
    def _(t):
        at = pl.ds(pl.multiple_of(t * ta, ta), ta)
        hi, lo = split(a_ref[at, :])
        a_hi[at, pl.ds(0, depth)] = hi
        a_lo[at, pl.ds(0, depth)] = lo

    order = [(0, 0), (half_ring, 0)]
    for s in range(half_ring - 1, 0, -1):
        order += [(s, -1), (s, 1)]
    blocks = []
    for s, way in order:
        blocks.append(lax.rem(c + (s if way >= 0 else C - s), C))

    def plane_copy(i, m):
        ref = gath.at[blocks[i], g, mine]
        return remote(ref, ref, s2.at[i, m - 1], r2.at[i, m - 1], lax.rem(j + m, C) * G + g, c)

    def plane_wait(i, m):
        from_j = lax.rem(j + C - m, C)
        ref = gath.at[blocks[i], g, pl.ds(pl.multiple_of(from_j * chunk, chunk), chunk)]
        remote(ref, ref, s2.at[i, m - 1], r2.at[i, m - 1], row, c).wait_recv()

    def group_copy(i, n):
        ref = gath.at[blocks[i], g]
        return remote(ref, ref, s3.at[i, n - 1], r3.at[i, n - 1], j * G + lax.rem(g + n, G), c)

    def group_wait(i, n):
        ref = gath.at[blocks[i], lax.rem(g + G - n, G)]
        remote(ref, ref, s3.at[i, n - 1], r3.at[i, n - 1], row, c).wait_recv()

    for i, (s, way) in enumerate(order):
        if s:
            m = C - s if way >= 0 else s
            ref = gath.at[blocks[i], g, mine]
            remote(ref, ref, s1.at[m - 1], r1.at[m - 1], row, c).wait_recv()
        else:
            keep.wait()
        for m in range(1, C):
            plane_copy(i, m).start()

    tb = row_tile(rows, 128)
    tm = row_tile(rows, 256)

    def multiply(i):
        q = blocks[i]
        for gg in range(G):
            @pl.loop(0, rows // tb)
            def _(t):
                hi, lo = split(gath[q, gg, pl.ds(pl.multiple_of(t * tb, tb), tb), :])
                at = pl.ds(pl.multiple_of(gg * rows + t * tb, tb), tb)
                b_hi[at, :] = hi
                b_lo[at, :] = lo

        @pl.loop(0, rows // tm)
        def _(t):
            at = pl.ds(pl.multiple_of(t * tm, tm), tm)
            dot = functools.partial(jnp.dot, preferred_element_type=jnp.float32)
            x_hi, x_lo = a_hi[at, pl.ds(0, depth)], a_lo[at, pl.ds(0, depth)]
            y_hi, y_lo = b_hi[pl.ds(0, depth), :], b_lo[pl.ds(0, depth), :]
            part[i, at, :] = dot(x_hi, y_lo) + dot(x_lo, y_hi) + dot(x_hi, y_hi)

    def ring_copy(i, way, s):
        to = lax.rem(c + (C - 1 if way == 0 else 1), C)
        piece = pl.ds(way * half, half) if s == half_ring else pl.ds(0, rows)
        return remote(
            part.at[i, piece], recv.at[way, s - 1, piece],
            s4.at[way, s - 1], r4.at[way, s - 1], row, to,
        )

    def ring_wait(way, s):
        piece = pl.ds(way * half, half) if s + 1 == half_ring else pl.ds(0, rows)
        ref = recv.at[way, s, piece]
        remote(ref, ref, s4.at[way, s], r4.at[way, s], row, c).wait_recv()

    def accumulate(i, way, s):
        lo, n = (way * half, half) if s + 1 == half_ring else (0, rows)
        step = row_tile(n, 128)

        @pl.loop(0, n // step)
        def _(t):
            at = pl.ds(pl.multiple_of(lo + t * step, 16), step)
            part[i, at, :] = part[i, at, :] + recv[way, s, at, :]

    sends = []
    for i, (s, way) in enumerate(order):
        for m in range(1, C):
            plane_wait(i, m)
        for n in range(1, G):
            group_copy(i, n).start()
        for n in range(1, G):
            group_wait(i, n)
        multiply(i)
        if s == half_ring:
            ways = (0, 1)
        elif s:
            ways = (0,) if way < 0 else (1,)
        else:
            ways = ()
        for w in ways:
            if s < half_ring:
                ring_wait(w, s)
                accumulate(i, w, s)
            copy = ring_copy(i, w, s)
            copy.start()
            sends.append(copy)

    ring_wait(0, 0)
    ring_wait(1, 0)

    @pl.loop(0, rows // ta)
    def _(t):
        at = pl.ds(pl.multiple_of(t * ta, ta), ta)
        x = part[0, at, :] + recv[0, 0, at, :] + recv[1, 0, at, :]
        out_ref[at, :] = x
        hi, lo = split(x)
        b_hi[at, :] = hi
        b_lo[at, :] = lo
        hi, lo = split(left_ref[at, :])
        a_hi[at, pl.ds(0, W)] = hi
        a_lo[at, pl.ds(0, W)] = lo

    for t in range(W // 128):
        at = pl.ds(t * 128, 128)
        dot = functools.partial(
            lax.dot_general, dimension_numbers=(((0,), (0,)), ((), ())),
            preferred_element_type=jnp.float32,
        )
        p_hi, p_lo = b_hi[pl.ds(0, rows), :], b_lo[pl.ds(0, rows), :]
        x = dot(a_hi[:, at], p_lo) + dot(a_lo[:, at], p_hi)
        gram[at, :] = x + dot(a_hi[:, at], p_hi)

    share = W // R

    def gram_copy(m):
        to = lax.rem(row + m, R)
        src = gram.at[pl.ds(pl.multiple_of(to * share, 8), share)]
        return remote(src, inbox.at[m - 1], s5.at[m - 1], r5.at[m - 1], to, c)

    for m in range(1, R):
        gram_copy(m).start()
    total = gram[pl.ds(pl.multiple_of(row * share, 8), share), :]
    for m in range(1, R):
        gram_copy(m).wait_recv()
        total = total + inbox[m - 1]
    gram_ref[...] = total

    for copy in sends:
        copy.wait_send()
    for m in range(1, C):
        spread_copy(m).wait_send()
        column_copy(lax.rem(c + m, C), m).wait_send()
    for m in range(1, R):
        gram_copy(m).wait_send()
    for i in range(C):
        for m in range(1, C):
            plane_copy(i, m).wait_send()
        for n in range(1, G):
            group_copy(i, n).wait_send()


def grid_product(R, C, a, l, left):
    rows, cols = l.shape
    G = R // C
    depth = a.shape[1]
    vmem = pl.BlockSpec(memory_space=pltpu.VMEM)
    dma = pltpu.SemaphoreType.DMA
    return pl.pallas_call(
        functools.partial(product_kernel, R, C),
        out_shape=[
            jax.ShapeDtypeStruct((rows, cols), jnp.float32),
            jax.ShapeDtypeStruct((W // R, cols), jnp.float32),
        ],
        in_specs=[vmem, vmem, vmem],
        out_specs=[vmem, vmem],
        scratch_shapes=[
            pltpu.VMEM((C, rows // C, cols), jnp.float32),
            pltpu.VMEM((C, G, rows, cols), jnp.float32),
            pltpu.VMEM((C, rows, cols), jnp.float32),
            pltpu.VMEM((2, C // 2, rows, cols), jnp.float32),
            pltpu.VMEM((W, cols), jnp.float32),
            pltpu.VMEM((R - 1, W // R, cols), jnp.float32),
            pltpu.VMEM((rows, max(depth, W)), jnp.bfloat16),
            pltpu.VMEM((rows, max(depth, W)), jnp.bfloat16),
            pltpu.VMEM((max(depth, rows), cols), jnp.bfloat16),
            pltpu.VMEM((max(depth, rows), cols), jnp.bfloat16),
            dma((C - 1,)),
            dma((C - 1,)),
            dma((C - 1,)),
            dma((C - 1,)),
            dma((C, C - 1)),
            dma((C, C - 1)),
            dma((C, max(G - 1, 1))),
            dma((C, max(G - 1, 1))),
            dma((2, C // 2)),
            dma((2, C // 2)),
            dma((R - 1,)),
            dma((R - 1,)),
            dma((2,)),
        ],
        compiler_params=pltpu.CompilerParams(
            collective_id=0, has_side_effects=True, vmem_limit_bytes=67043328
        ),
    )(a, l, left)


def pieces_of(tiles):
    sizes = [1]
    while sum(sizes) < tiles:
        sizes.append(2 if tiles - sum(sizes) > 2 else 1)
    return [(sum(sizes[:p]), n) for p, n in enumerate(sizes)]


def line_kernel(
    R, C, a_hbm, f_hbm, diag_ref, widths_ref, member_ref, out_ref, dout_ref,
    a_raw, mask, lm, mid, gath, part, recv, a_hi, a_lo, b_hi, b_lo, t_hi, t_lo,
    gram, inbox, in_sem, own_sem, s0, r0, s1, r1, s2, r2, s3, r3, s4, r4, s5, r5, s6, r6,
):
    rows, depth = a_raw.shape
    tiles = lm.shape[0]
    G = R // C
    chunk = rows // C
    half = chunk // 2
    share = W // R
    pieces = pieces_of(tiles)
    row = lax.axis_index("row")
    c = lax.axis_index("col")
    j = row // G
    g = lax.rem(row, G)
    other = 1 - g
    jx = j + 1 - 2 * lax.rem(j, 2)
    jy = lax.rem(j + 2, C)
    jd = C - 1 - j
    last = C - 1
    h = c // 2
    m = c + h * (last - 2 * c)

    def flip(n):
        return n + h * (last - 2 * n)

    blocks = [flip(3), flip(2 - 2 * m), flip(1 + m), c]
    onward = [flip(m + 1), flip(1 - m), flip(m + 1)]
    slots = [blocks[0], blocks[1], blocks[2] + m * (C - blocks[2])]

    def load_f(t):
        return pltpu.make_async_copy(f_hbm.at[:, pl.ds(t * 128, 128)], lm.at[t], in_sem.at[t])

    load_a = pltpu.make_async_copy(a_hbm, a_raw, in_sem.at[tiles])
    for t in range(tiles):
        load_f(t).start()
    load_a.start()

    barrier = pltpu.get_barrier_semaphore()

    def greet(r, q):
        pl.semaphore_signal(barrier, inc=1, device_id=(r, q), device_id_type=MESH)

    for n in range(1, R):
        greet(lax.rem(row + n, R), c)

    for n in range(1, C):
        greet(row, lax.rem(c + n, C))

    keep = lax.broadcasted_iota(jnp.int32, (NODES, 128), 0) == c
    width = widths_ref[c]
    member = member_ref[...].astype(jnp.float32).astype(jnp.bfloat16)

    def make_mask(t):
        q = lax.broadcasted_iota(jnp.int32, (NODES, 128), 1) + t * 128
        pick = jnp.where(keep & (q < width), 1.0, 0.0).astype(jnp.bfloat16)
        x = lax.dot_general(
            member, pick, (((0,), (0,)), ((), ())), preferred_element_type=jnp.float32
        )
        load_f(t).wait()
        mask[t] = x
        lm[t] = lm[t] * x

    for t in range(pieces[0][1]):
        make_mask(t)

    pl.semaphore_wait(barrier, R + C - 2)

    def remote(src, dst, ssem, rsem, r, q):
        return pltpu.make_async_remote_copy(
            src_ref=src, dst_ref=dst, send_sem=ssem, recv_sem=rsem,
            device_id=(r, q), device_id_type=MESH,
        )

    def at_tiles(p):
        t, n = pieces[p]
        return pl.ds(t, n)

    def spot(gg, jj, n=None, k=0):
        start = gg * rows + jj * chunk + k * half
        return pl.ds(pl.multiple_of(start, 8), half if n else chunk)

    mine = pl.ds(pl.multiple_of(j * chunk, 8), chunk)
    near = [j, jx, jy, jd]

    def spread_copy(d, p):
        src = lm.at[at_tiles(p), pl.ds(pl.multiple_of(near[d] * chunk, 8), chunk)]
        dst = mid.at[d - 1, at_tiles(p)]
        return remote(src, dst, s0.at[d - 1, p], r0.at[d - 1, p], near[d] * G + g, c)

    def spread_start(p):
        for d in range(1, C):
            spread_copy(d, p).start()

    def line_source(d, p):
        return mid.at[d - 1, at_tiles(p)] if d else lm.at[at_tiles(p), mine]

    def line_copy(d, p):
        dst = gath.at[c, at_tiles(p), spot(g, j)]
        return remote(line_source(d, p), dst, s6.at[d, p], r6.at[c, p], row, near[d])

    def keep_copy(d, p):
        dst = gath.at[c, at_tiles(p), spot(g, j)]
        return pltpu.make_async_copy(line_source(d, p), dst, own_sem.at[p])

    def line_start(d, p):
        if d:
            spread_copy(d, p).wait_recv()

        @pl.when(near[d] != c)
        def _():
            line_copy(d, p).start()

        @pl.when(near[d] == c)
        def _():
            keep_copy(d, p).start()

    def line_sent(p):
        for d in range(C):
            @pl.when(near[d] != c)
            def _():
                line_copy(d, p).wait_send()

    spread_start(0)
    line_start(0, 0)
    for t in range(pieces[0][1], tiles):
        make_mask(t)
    for p in range(1, len(pieces)):
        line_start(0, p)
    for d in range(1, C):
        line_start(d, 0)
    for p in range(1, len(pieces)):
        spread_start(p)
    load_a.wait()
    ta = row_tile(rows, 128)

    @pl.loop(0, rows // ta)
    def _(t):
        at = pl.ds(pl.multiple_of(t * ta, ta), ta)
        hi, lo = split(a_raw[at, :])
        a_hi[at, :] = hi
        a_lo[at, :] = lo

    for t in range(tiles):
        hi, lo = split(lm[t].T)
        t_hi[pl.ds(t * 128, 128), :] = hi
        t_lo[pl.ds(t * 128, 128), :] = lo

    for p in range(1, len(pieces)):
        for d in range(1, C):
            line_start(d, p)
    units = [(i, p) for p in range(len(pieces)) for i in range(C)]

    def take(u):
        i, p = units[u]
        if i == C - 1:
            keep_copy(0, p).wait()
        else:
            ref = gath.at[blocks[i], at_tiles(p), spot(g, j)]
            remote(ref, ref, s6.at[0, p], r6.at[blocks[i], p], row, c).wait_recv()

    def pass_copy(u, way):
        i, p = units[u]
        ref = gath.at[blocks[i], at_tiles(p), spot(g, j)]
        to = jx if way == 0 else jy
        return remote(ref, ref, s1.at[u, way], r1.at[u, way], to * G + g, c)

    def pass_wait(u, way):
        i, p = units[u]
        ref = gath.at[blocks[i], at_tiles(p), spot(g, jx if way == 0 else jy)]
        remote(ref, ref, s1.at[u, way], r1.at[u, way], row, c).wait_recv()

    def forward_copy(u, way):
        i, p = units[u]
        ref = gath.at[blocks[i], at_tiles(p), spot(g, jx if way == 0 else jy, 1, way)]
        to = jy if way == 0 else jx
        return remote(ref, ref, s2.at[u, way], r2.at[u, way], to * G + g, c)

    def forward_wait(u, way):
        i, p = units[u]
        ref = gath.at[blocks[i], at_tiles(p), spot(g, jd, 1, way)]
        remote(ref, ref, s2.at[u, way], r2.at[u, way], row, c).wait_recv()

    def swap_copy(u):
        i, p = units[u]
        ref = gath.at[blocks[i], at_tiles(p), pl.ds(pl.multiple_of(g * rows, 8), rows)]
        return remote(ref, ref, s3.at[u], r3.at[u], j * G + other, c)

    def swap_wait(u):
        i, p = units[u]
        ref = gath.at[blocks[i], at_tiles(p), pl.ds(pl.multiple_of(other * rows, 8), rows)]
        remote(ref, ref, s3.at[u], r3.at[u], row, c).wait_recv()

    def sum_copy(u):
        i, p = units[u]
        return remote(
            part.at[i, at_tiles(p)], recv.at[slots[i], at_tiles(p)],
            s4.at[i, p], r4.at[slots[i], p], row, onward[i],
        )

    def sum_wait(slot, p):
        ref = recv.at[slot, at_tiles(p)]
        remote(ref, ref, s4.at[0, p], r4.at[slot, p], row, c).wait_recv()

    def stage_a(u):
        take(u)
        for way in range(2):
            pass_copy(u, way).start()

    def stage_b(u):
        for way in range(2):
            pass_wait(u, way)
            forward_copy(u, way).start()

    def stage_c(u):
        for way in range(2):
            forward_wait(u, way)
        swap_copy(u).start()

    tb = row_tile(depth, 256)
    tm = row_tile(rows, 384)

    def stage_d(u):
        i, p = units[u]
        t0, n = pieces[p]
        q = blocks[i]
        cols = pl.ds(0, n * 128)
        swap_wait(u)

        @pl.loop(0, depth // tb)
        def _(t):
            at = pl.ds(pl.multiple_of(t * tb, tb), tb)
            for k in range(n):
                hi, lo = split(gath[q, t0 + k, at, :])
                b_hi[at, pl.ds(k * 128, 128)] = hi
                b_lo[at, pl.ds(k * 128, 128)] = lo

        @pl.loop(0, rows // tm)
        def _(t):
            at = pl.ds(pl.multiple_of(t * tm, tm), tm)
            dot = functools.partial(jnp.dot, preferred_element_type=jnp.float32)
            x = dot(a_hi[at, :], b_lo[:, cols]) + dot(a_lo[at, :], b_hi[:, cols])
            x = x + dot(a_hi[at, :], b_hi[:, cols])
            for k in range(n):
                part[i, t0 + k, at, :] = x[:, k * 128:(k + 1) * 128]

        if i < C - 1:
            @pl.when(m == 0)
            def _():
                if len(in_flight) == 2:
                    sum_copy(in_flight[0]).wait_send()
                sum_copy(u).start()

            if len(in_flight) == 2:
                in_flight.pop(0)
            in_flight.append(u)

    def add_in(i, slot, p):
        t0, n = pieces[p]

        @pl.loop(0, rows // ta)
        def _(t):
            at = pl.ds(pl.multiple_of(t * ta, ta), ta)
            for k in range(n):
                part[i, t0 + k, at, :] = part[i, t0 + k, at, :] + recv[slot, t0 + k, at, :]

    def stage_e(u):
        i, p = units[u]

        @pl.when(m == 1)
        def _():
            sum_wait(blocks[i], p)
            add_in(i, blocks[i], p)
            sum_copy(u).start()

    def gram_copy(n, p):
        to = lax.rem(row + n, R)
        return remote(
            gram.at[at_tiles(p), to], inbox.at[n - 1, at_tiles(p)],
            s5.at[n - 1, p], r5.at[n - 1, p], to, c,
        )

    def stage_f(p):
        t0, n = pieces[p]
        cols = pl.ds(0, n * 128)

        @pl.when(m == 1)
        def _():
            sum_wait(C, p)
            add_in(C - 1, C, p)

        sum_wait(c, p)

        @pl.loop(0, rows // ta)
        def _(t):
            at = pl.ds(pl.multiple_of(t * ta, ta), ta)
            for k in range(n):
                x = part[C - 1, t0 + k, at, :] + recv[c, t0 + k, at, :]
                out_ref[at, pl.ds((t0 + k) * 128, 128)] = -x * mask[t0 + k, at, :]
                hi, lo = split(x)
                b_hi[at, pl.ds(k * 128, 128)] = hi
                b_lo[at, pl.ds(k * 128, 128)] = lo

        dot = functools.partial(jnp.dot, preferred_element_type=jnp.float32)
        p_hi, p_lo = b_hi[pl.ds(0, rows), cols], b_lo[pl.ds(0, rows), cols]
        for r in range(0, R, 4):
            at = pl.ds(r * share, 4 * share)
            x = dot(t_hi[at, :], p_lo) + dot(t_lo[at, :], p_hi) + dot(t_hi[at, :], p_hi)
            for e in range(4):
                for k in range(n):
                    gram[t0 + k, r + e] = x[e * share:(e + 1) * share, k * 128:(k + 1) * 128]
        for k in range(1, R):
            gram_copy(k, p).start()

    def stage_g(p):
        t0, n = pieces[p]
        for k in range(1, R):
            gram_copy(k, p).wait_recv()
        for k in range(n):
            t = t0 + k
            x = gram[t, row]
            for d in range(R - 1):
                x = x + inbox[d, t]
            at = pl.ds(t * 128, 128)
            r = lax.broadcasted_iota(jnp.int32, (share, 128), 0) + row * share
            q = lax.broadcasted_iota(jnp.int32, (share, 128), 1) + t * 128
            inside = (r < width) & (q < width)
            dout_ref[:, at] = jnp.where(inside, diag_ref[:, at] + x, 0.0)

    total = len(units)
    finished = 0
    in_flight = []
    for step in range(total + 5):
        u = step - 5
        if u >= 0:
            i, p = units[u]
            if i < C - 1:
                stage_e(u)
            if p and i == (0 if p == len(pieces) - 1 else C - 2):
                stage_f(p - 1)
                finished = p
        if 0 <= step - 3 < total:
            stage_d(step - 3)
        if 0 <= step - 2 < total:
            stage_c(step - 2)
        if 0 <= step - 1 < total:
            stage_b(step - 1)
        if step < total:
            stage_a(step)
    for p in range(finished, len(pieces)):
        stage_f(p)
    for p in range(len(pieces)):
        stage_g(p)

    for p in range(len(pieces)):
        line_sent(p)
        for d in range(1, C):
            spread_copy(d, p).wait_send()
        for k in range(1, R):
            gram_copy(k, p).wait_send()
    for u in range(total):
        for way in range(2):
            pass_copy(u, way).wait_send()
            forward_copy(u, way).wait_send()
        swap_copy(u).wait_send()

    @pl.when(m == 0)
    def _():
        for u in in_flight:
            sum_copy(u).wait_send()

    @pl.when(m == 1)
    def _():
        for u in range(total):
            if units[u][0] < C - 1:
                sum_copy(u).wait_send()


def line_product(R, C, a, f, diag, widths, member):
    rows, depth = a.shape
    cols = f.shape[1]
    tiles = cols // 128
    pieces = len(pieces_of(tiles))
    units = C * pieces
    f32, bf16 = jnp.float32, jnp.bfloat16
    vmem = pl.BlockSpec(memory_space=pltpu.VMEM)
    smem = pl.BlockSpec(memory_space=pltpu.SMEM)
    hbm = pl.BlockSpec(memory_space=pl.ANY)
    dma = pltpu.SemaphoreType.DMA
    return pl.pallas_call(
        functools.partial(line_kernel, R, C),
        out_shape=[
            jax.ShapeDtypeStruct((rows, cols), f32),
            jax.ShapeDtypeStruct((W // R, cols), f32),
        ],
        in_specs=[hbm, hbm, vmem, smem, vmem],
        out_specs=[vmem, vmem],
        scratch_shapes=[
            pltpu.VMEM((rows, depth), f32),
            pltpu.VMEM((tiles, rows, 128), f32),
            pltpu.VMEM((tiles, rows, 128), f32),
            pltpu.VMEM((C - 1, tiles, rows // C, 128), f32),
            pltpu.VMEM((C, tiles, depth, 128), f32),
            pltpu.VMEM((C, tiles, rows, 128), f32),
            pltpu.VMEM((C + 1, tiles, rows, 128), f32),
            pltpu.VMEM((rows, depth), bf16),
            pltpu.VMEM((rows, depth), bf16),
            pltpu.VMEM((depth, 256), bf16),
            pltpu.VMEM((depth, 256), bf16),
            pltpu.VMEM((W, rows), bf16),
            pltpu.VMEM((W, rows), bf16),
            pltpu.VMEM((tiles, R, W // R, 128), f32),
            pltpu.VMEM((R - 1, tiles, W // R, 128), f32),
            dma((tiles + 1,)),
            dma((pieces,)),
            dma((C - 1, pieces)),
            dma((C - 1, pieces)),
            dma((units, 2)),
            dma((units, 2)),
            dma((units, 2)),
            dma((units, 2)),
            dma((units,)),
            dma((units,)),
            dma((C - 1, pieces)),
            dma((C + 1, pieces)),
            dma((R - 1, pieces)),
            dma((R - 1, pieces)),
            dma((C, pieces)),
            dma((C, pieces)),
        ],
        compiler_params=pltpu.CompilerParams(
            collective_id=1, has_side_effects=True, vmem_limit_bytes=67043328
        ),
    )(a, f, diag, widths, member)


def per_device(ancestor_inverse, factor, diag_inverse, widths, member):
    R = lax.axis_size("row")
    C = lax.axis_size("col")
    my_row = lax.axis_index("row")
    my_col = lax.axis_index("col")
    shard_cols = factor.shape[1]
    rows, depth = ancestor_inverse.shape
    if C == NODES and R == 2 * C and shard_cols == W and depth == 2 * rows:
        return tuple(line_product(R, C, ancestor_inverse, factor, diag_inverse, widths, member))
    col_start = my_col * shard_cols
    global_cols = col_start + jnp.arange(shard_cols, dtype=jnp.int32)
    node_of = global_cols // W
    within = global_cols % W
    select = node_of[None, :] == jnp.arange(NODES, dtype=jnp.int32)[:, None]
    width_col = jnp.sum(jnp.where(select, widths[:, None], 0), axis=0)
    col_keep = within < width_col
    pick = jnp.where(select & col_keep[None, :], 1.0, 0.0).astype(jnp.bfloat16)
    mask = lax.dot_general(
        member.astype(jnp.bfloat16), pick, (((0,), (0,)), ((), ())),
        preferred_element_type=jnp.float32,
    )
    masked = factor * mask
    if shard_cols == W:
        left = masked
    else:
        rows_full = lax.all_gather(masked, "col", axis=1, tiled=True)
        left = lax.dynamic_slice_in_dim(rows_full, col_start // W * W, W, 1)
    product, gram = grid_product(R, C, ancestor_inverse, masked, left)
    offdiag = -product * mask
    diag_rows = diag_inverse.shape[0]
    local_rows = my_row * diag_rows + jnp.arange(diag_rows, dtype=jnp.int32)
    inside = (local_rows[:, None] < width_col[None, :]) & col_keep[None, :]
    diag_blocks = (diag_inverse + gram) * inside.astype(jnp.float32)
    return (offdiag, diag_blocks)


def solution(mesh):
    in_specs = (P("row", "col"), P("row", "col"), P("row", "col"), P(), P(None, "row"))
    out_specs = (P("row", "col"), P("row", "col"))
    return jax.shard_map(
        per_device, mesh=mesh, in_specs=in_specs, out_specs=out_specs, check_vma=False
    )
```

```python
import functools

import jax
import jax.numpy as jnp
from jax import lax
from jax.experimental import pallas as pl
from jax.experimental.pallas import tpu as pltpu
from jax.sharding import PartitionSpec as P

W = 640
NODES = 4
MESH = pl.DeviceIdType.MESH


def split(x):
    hi = x.astype(jnp.bfloat16)
    lo = (x - hi.astype(jnp.float32)).astype(jnp.bfloat16)
    return hi, lo


def row_tile(rows, most):
    return max(t for t in range(16, most + 1, 16) if rows % t == 0)


def product_kernel(
    R, C, a_ref, l_ref, left_ref, out_ref, gram_ref, mid, gath, part, recv, gram, inbox,
    a_hi, a_lo, b_hi, b_lo, s0, r0, s1, r1, s2, r2, s3, r3, s4, r4, s5, r5, own_sem,
):
    G = R // C
    half_ring = C // 2
    row = lax.axis_index("row")
    c = lax.axis_index("col")
    j = row // G
    g = lax.rem(row, G)
    rows, cols = l_ref.shape
    depth = a_ref.shape[1]
    chunk = rows // C
    half = rows // 2

    barrier = pltpu.get_barrier_semaphore()

    def greet(r, q):
        pl.semaphore_signal(barrier, inc=1, device_id=(r, q), device_id_type=MESH)

    for m in range(1, R):
        greet(lax.rem(row + m, R), c)
    for m in range(1, C):
        greet(row, lax.rem(c + m, C))
    pl.semaphore_wait(barrier, R + C - 2)

    def remote(src, dst, ssem, rsem, r, q):
        return pltpu.make_async_remote_copy(
            src_ref=src, dst_ref=dst, send_sem=ssem, recv_sem=rsem,
            device_id=(r, q), device_id_type=MESH,
        )

    mine = pl.ds(pl.multiple_of(j * chunk, chunk), chunk)

    def spread_copy(m):
        n = lax.rem(j + m, C)
        src = l_ref.at[pl.ds(pl.multiple_of(n * chunk, chunk), chunk)]
        return remote(src, mid.at[j], s0.at[m - 1], r0.at[m - 1], n * G + g, c)

    def column_copy(p, m):
        return remote(
            mid.at[p], gath.at[c, g, mine], s1.at[m - 1], r1.at[m - 1], row, p
        )

    for m in range(1, C):
        spread_copy(m).start()
    own = pltpu.make_async_copy(l_ref.at[mine], mid.at[j], own_sem.at[0])
    own.start()
    own.wait()
    for m in range(1, C):
        ref = mid.at[lax.rem(j + C - m, C)]
        remote(ref, ref, s0.at[m - 1], r0.at[m - 1], row, c).wait_recv()
    ways_on = sorted(range(1, C), key=lambda m: -min(m, C - m))
    for m in ways_on:
        column_copy(lax.rem(c + m, C), m).start()
    keep = pltpu.make_async_copy(mid.at[c], gath.at[c, g, mine], own_sem.at[1])
    keep.start()

    ta = row_tile(rows, 128)

    @pl.loop(0, rows // ta)
    def _(t):
        at = pl.ds(pl.multiple_of(t * ta, ta), ta)
        hi, lo = split(a_ref[at, :])
        a_hi[at, pl.ds(0, depth)] = hi
        a_lo[at, pl.ds(0, depth)] = lo

    order = [(0, 0), (half_ring, 0)]
    for s in range(half_ring - 1, 0, -1):
        order += [(s, -1), (s, 1)]
    blocks = []
    for s, way in order:
        blocks.append(lax.rem(c + (s if way >= 0 else C - s), C))

    def plane_copy(i, m):
        ref = gath.at[blocks[i], g, mine]
        return remote(ref, ref, s2.at[i, m - 1], r2.at[i, m - 1], lax.rem(j + m, C) * G + g, c)

    def plane_wait(i, m):
        from_j = lax.rem(j + C - m, C)
        ref = gath.at[blocks[i], g, pl.ds(pl.multiple_of(from_j * chunk, chunk), chunk)]
        remote(ref, ref, s2.at[i, m - 1], r2.at[i, m - 1], row, c).wait_recv()

    def group_copy(i, n):
        ref = gath.at[blocks[i], g]
        return remote(ref, ref, s3.at[i, n - 1], r3.at[i, n - 1], j * G + lax.rem(g + n, G), c)

    def group_wait(i, n):
        ref = gath.at[blocks[i], lax.rem(g + G - n, G)]
        remote(ref, ref, s3.at[i, n - 1], r3.at[i, n - 1], row, c).wait_recv()

    for i, (s, way) in enumerate(order):
        if s:
            m = C - s if way >= 0 else s
            ref = gath.at[blocks[i], g, mine]
            remote(ref, ref, s1.at[m - 1], r1.at[m - 1], row, c).wait_recv()
        else:
            keep.wait()
        for m in range(1, C):
            plane_copy(i, m).start()

    tb = row_tile(rows, 128)
    tm = row_tile(rows, 256)

    def multiply(i):
        q = blocks[i]
        for gg in range(G):
            @pl.loop(0, rows // tb)
            def _(t):
                hi, lo = split(gath[q, gg, pl.ds(pl.multiple_of(t * tb, tb), tb), :])
                at = pl.ds(pl.multiple_of(gg * rows + t * tb, tb), tb)
                b_hi[at, :] = hi
                b_lo[at, :] = lo

        @pl.loop(0, rows // tm)
        def _(t):
            at = pl.ds(pl.multiple_of(t * tm, tm), tm)
            dot = functools.partial(jnp.dot, preferred_element_type=jnp.float32)
            x_hi, x_lo = a_hi[at, pl.ds(0, depth)], a_lo[at, pl.ds(0, depth)]
            y_hi, y_lo = b_hi[pl.ds(0, depth), :], b_lo[pl.ds(0, depth), :]
            part[i, at, :] = dot(x_hi, y_lo) + dot(x_lo, y_hi) + dot(x_hi, y_hi)

    def ring_copy(i, way, s):
        to = lax.rem(c + (C - 1 if way == 0 else 1), C)
        piece = pl.ds(way * half, half) if s == half_ring else pl.ds(0, rows)
        return remote(
            part.at[i, piece], recv.at[way, s - 1, piece],
            s4.at[way, s - 1], r4.at[way, s - 1], row, to,
        )

    def ring_wait(way, s):
        piece = pl.ds(way * half, half) if s + 1 == half_ring else pl.ds(0, rows)
        ref = recv.at[way, s, piece]
        remote(ref, ref, s4.at[way, s], r4.at[way, s], row, c).wait_recv()

    def accumulate(i, way, s):
        lo, n = (way * half, half) if s + 1 == half_ring else (0, rows)
        step = row_tile(n, 128)

        @pl.loop(0, n // step)
        def _(t):
            at = pl.ds(pl.multiple_of(lo + t * step, 16), step)
            part[i, at, :] = part[i, at, :] + recv[way, s, at, :]

    sends = []
    for i, (s, way) in enumerate(order):
        for m in range(1, C):
            plane_wait(i, m)
        for n in range(1, G):
            group_copy(i, n).start()
        for n in range(1, G):
            group_wait(i, n)
        multiply(i)
        if s == half_ring:
            ways = (0, 1)
        elif s:
            ways = (0,) if way < 0 else (1,)
        else:
            ways = ()
        for w in ways:
            if s < half_ring:
                ring_wait(w, s)
                accumulate(i, w, s)
            copy = ring_copy(i, w, s)
            copy.start()
            sends.append(copy)

    ring_wait(0, 0)
    ring_wait(1, 0)

    @pl.loop(0, rows // ta)
    def _(t):
        at = pl.ds(pl.multiple_of(t * ta, ta), ta)
        x = part[0, at, :] + recv[0, 0, at, :] + recv[1, 0, at, :]
        out_ref[at, :] = x
        hi, lo = split(x)
        b_hi[at, :] = hi
        b_lo[at, :] = lo
        hi, lo = split(left_ref[at, :])
        a_hi[at, pl.ds(0, W)] = hi
        a_lo[at, pl.ds(0, W)] = lo

    for t in range(W // 128):
        at = pl.ds(t * 128, 128)
        dot = functools.partial(
            lax.dot_general, dimension_numbers=(((0,), (0,)), ((), ())),
            preferred_element_type=jnp.float32,
        )
        p_hi, p_lo = b_hi[pl.ds(0, rows), :], b_lo[pl.ds(0, rows), :]
        x = dot(a_hi[:, at], p_lo) + dot(a_lo[:, at], p_hi)
        gram[at, :] = x + dot(a_hi[:, at], p_hi)

    share = W // R

    def gram_copy(m):
        to = lax.rem(row + m, R)
        src = gram.at[pl.ds(pl.multiple_of(to * share, 8), share)]
        return remote(src, inbox.at[m - 1], s5.at[m - 1], r5.at[m - 1], to, c)

    for m in range(1, R):
        gram_copy(m).start()
    total = gram[pl.ds(pl.multiple_of(row * share, 8), share), :]
    for m in range(1, R):
        gram_copy(m).wait_recv()
        total = total + inbox[m - 1]
    gram_ref[...] = total

    for copy in sends:
        copy.wait_send()
    for m in range(1, C):
        spread_copy(m).wait_send()
        column_copy(lax.rem(c + m, C), m).wait_send()
    for m in range(1, R):
        gram_copy(m).wait_send()
    for i in range(C):
        for m in range(1, C):
            plane_copy(i, m).wait_send()
        for n in range(1, G):
            group_copy(i, n).wait_send()


def grid_product(R, C, a, l, left):
    rows, cols = l.shape
    G = R // C
    depth = a.shape[1]
    vmem = pl.BlockSpec(memory_space=pltpu.VMEM)
    dma = pltpu.SemaphoreType.DMA
    return pl.pallas_call(
        functools.partial(product_kernel, R, C),
        out_shape=[
            jax.ShapeDtypeStruct((rows, cols), jnp.float32),
            jax.ShapeDtypeStruct((W // R, cols), jnp.float32),
        ],
        in_specs=[vmem, vmem, vmem],
        out_specs=[vmem, vmem],
        scratch_shapes=[
            pltpu.VMEM((C, rows // C, cols), jnp.float32),
            pltpu.VMEM((C, G, rows, cols), jnp.float32),
            pltpu.VMEM((C, rows, cols), jnp.float32),
            pltpu.VMEM((2, C // 2, rows, cols), jnp.float32),
            pltpu.VMEM((W, cols), jnp.float32),
            pltpu.VMEM((R - 1, W // R, cols), jnp.float32),
            pltpu.VMEM((rows, max(depth, W)), jnp.bfloat16),
            pltpu.VMEM((rows, max(depth, W)), jnp.bfloat16),
            pltpu.VMEM((max(depth, rows), cols), jnp.bfloat16),
            pltpu.VMEM((max(depth, rows), cols), jnp.bfloat16),
            dma((C - 1,)),
            dma((C - 1,)),
            dma((C - 1,)),
            dma((C - 1,)),
            dma((C, C - 1)),
            dma((C, C - 1)),
            dma((C, max(G - 1, 1))),
            dma((C, max(G - 1, 1))),
            dma((2, C // 2)),
            dma((2, C // 2)),
            dma((R - 1,)),
            dma((R - 1,)),
            dma((2,)),
        ],
        compiler_params=pltpu.CompilerParams(
            collective_id=0, has_side_effects=True, vmem_limit_bytes=67043328
        ),
    )(a, l, left)


def pieces_of(tiles):
    sizes = [1]
    while sum(sizes) < tiles:
        sizes.append(2 if tiles - sum(sizes) > 2 else 1)
    return [(sum(sizes[:p]), n) for p, n in enumerate(sizes)]


def line_kernel(
    R, C, a_hbm, f_hbm, diag_ref, widths_ref, member_ref, out_ref, dout_ref,
    a_raw, mask, lm, mid, gath, part, recv, a_hi, a_lo, b_hi, b_lo, t_hi, t_lo,
    gram, inbox, in_sem, own_sem, s0, r0, s1, r1, s2, r2, s3, r3, s4, r4, s5, r5, s6, r6,
):
    rows, depth = a_raw.shape
    tiles = lm.shape[0]
    G = R // C
    chunk = rows // C
    half = chunk // 2
    share = W // R
    pieces = pieces_of(tiles)
    row = lax.axis_index("row")
    c = lax.axis_index("col")
    j = row // G
    g = lax.rem(row, G)
    other = 1 - g
    jx = j + 1 - 2 * lax.rem(j, 2)
    jy = lax.rem(j + 2, C)
    jd = C - 1 - j
    last = C - 1
    h = c // 2
    m = c + h * (last - 2 * c)

    def flip(n):
        return n + h * (last - 2 * n)

    blocks = [flip(3), flip(2 - 2 * m), flip(1 + m), c]
    onward = [flip(m + 1), flip(1 - m), flip(m + 1)]
    slots = [blocks[0], blocks[1], blocks[2] + m * (C - blocks[2])]

    def load_f(t):
        return pltpu.make_async_copy(f_hbm.at[:, pl.ds(t * 128, 128)], lm.at[t], in_sem.at[t])

    load_a = pltpu.make_async_copy(a_hbm, a_raw, in_sem.at[tiles])
    for t in range(tiles):
        load_f(t).start()
    load_a.start()

    barrier = pltpu.get_barrier_semaphore()

    def greet(r, q):
        pl.semaphore_signal(barrier, inc=1, device_id=(r, q), device_id_type=MESH)

    for n in range(1, R):
        greet(lax.rem(row + n, R), c)

    for n in range(1, C):
        greet(row, lax.rem(c + n, C))

    keep = lax.broadcasted_iota(jnp.int32, (NODES, 128), 0) == c
    width = widths_ref[c]
    member = member_ref[...].astype(jnp.float32).astype(jnp.bfloat16)

    def make_mask(t):
        q = lax.broadcasted_iota(jnp.int32, (NODES, 128), 1) + t * 128
        pick = jnp.where(keep & (q < width), 1.0, 0.0).astype(jnp.bfloat16)
        x = lax.dot_general(
            member, pick, (((0,), (0,)), ((), ())), preferred_element_type=jnp.float32
        )
        load_f(t).wait()
        mask[t] = x
        lm[t] = lm[t] * x

    for t in range(pieces[0][1]):
        make_mask(t)

    pl.semaphore_wait(barrier, R + C - 2)

    def remote(src, dst, ssem, rsem, r, q):
        return pltpu.make_async_remote_copy(
            src_ref=src, dst_ref=dst, send_sem=ssem, recv_sem=rsem,
            device_id=(r, q), device_id_type=MESH,
        )

    def at_tiles(p):
        t, n = pieces[p]
        return pl.ds(t, n)

    def spot(gg, jj, n=None, k=0):
        start = gg * rows + jj * chunk + k * half
        return pl.ds(pl.multiple_of(start, 8), half if n else chunk)

    mine = pl.ds(pl.multiple_of(j * chunk, 8), chunk)
    near = [j, jx, jy, jd]

    def spread_copy(d, p):
        src = lm.at[at_tiles(p), pl.ds(pl.multiple_of(near[d] * chunk, 8), chunk)]
        dst = mid.at[d - 1, at_tiles(p)]
        return remote(src, dst, s0.at[d - 1, p], r0.at[d - 1, p], near[d] * G + g, c)

    def spread_start(p):
        for d in range(1, C):
            spread_copy(d, p).start()

    def line_source(d, p):
        return mid.at[d - 1, at_tiles(p)] if d else lm.at[at_tiles(p), mine]

    def line_copy(d, p):
        dst = gath.at[c, at_tiles(p), spot(g, j)]
        return remote(line_source(d, p), dst, s6.at[d, p], r6.at[c, p], row, near[d])

    def keep_copy(d, p):
        dst = gath.at[c, at_tiles(p), spot(g, j)]
        return pltpu.make_async_copy(line_source(d, p), dst, own_sem.at[p])

    def line_start(d, p):
        if d:
            spread_copy(d, p).wait_recv()

        @pl.when(near[d] != c)
        def _():
            line_copy(d, p).start()

        @pl.when(near[d] == c)
        def _():
            keep_copy(d, p).start()

    def line_sent(p):
        for d in range(C):
            @pl.when(near[d] != c)
            def _():
                line_copy(d, p).wait_send()

    spread_start(0)
    line_start(0, 0)
    for t in range(pieces[0][1], tiles):
        make_mask(t)
    for d in range(1, C):
        line_start(d, 0)
    for p in range(1, len(pieces)):
        spread_start(p)
    for p in range(1, len(pieces)):
        line_start(0, p)
    load_a.wait()
    ta = row_tile(rows, 128)

    @pl.loop(0, rows // ta)
    def _(t):
        at = pl.ds(pl.multiple_of(t * ta, ta), ta)
        hi, lo = split(a_raw[at, :])
        a_hi[at, :] = hi
        a_lo[at, :] = lo

    for t in range(tiles):
        hi, lo = split(lm[t].T)
        t_hi[pl.ds(t * 128, 128), :] = hi
        t_lo[pl.ds(t * 128, 128), :] = lo

    for p in range(1, len(pieces)):
        for d in range(1, C):
            line_start(d, p)
    units = [(i, p) for p in range(len(pieces)) for i in range(C)]

    def take(u):
        i, p = units[u]
        if i == C - 1:
            keep_copy(0, p).wait()
        else:
            ref = gath.at[blocks[i], at_tiles(p), spot(g, j)]
            remote(ref, ref, s6.at[0, p], r6.at[blocks[i], p], row, c).wait_recv()

    def pass_copy(u, way):
        i, p = units[u]
        ref = gath.at[blocks[i], at_tiles(p), spot(g, j)]
        to = jx if way == 0 else jy
        return remote(ref, ref, s1.at[u, way], r1.at[u, way], to * G + g, c)

    def pass_wait(u, way):
        i, p = units[u]
        ref = gath.at[blocks[i], at_tiles(p), spot(g, jx if way == 0 else jy)]
        remote(ref, ref, s1.at[u, way], r1.at[u, way], row, c).wait_recv()

    def forward_copy(u, way):
        i, p = units[u]
        ref = gath.at[blocks[i], at_tiles(p), spot(g, jx if way == 0 else jy, 1, way)]
        to = jy if way == 0 else jx
        return remote(ref, ref, s2.at[u, way], r2.at[u, way], to * G + g, c)

    def forward_wait(u, way):
        i, p = units[u]
        ref = gath.at[blocks[i], at_tiles(p), spot(g, jd, 1, way)]
        remote(ref, ref, s2.at[u, way], r2.at[u, way], row, c).wait_recv()

    def swap_copy(u):
        i, p = units[u]
        ref = gath.at[blocks[i], at_tiles(p), pl.ds(pl.multiple_of(g * rows, 8), rows)]
        return remote(ref, ref, s3.at[u], r3.at[u], j * G + other, c)

    def swap_wait(u):
        i, p = units[u]
        ref = gath.at[blocks[i], at_tiles(p), pl.ds(pl.multiple_of(other * rows, 8), rows)]
        remote(ref, ref, s3.at[u], r3.at[u], row, c).wait_recv()

    def sum_copy(u):
        i, p = units[u]
        return remote(
            part.at[i, at_tiles(p)], recv.at[slots[i], at_tiles(p)],
            s4.at[i, p], r4.at[slots[i], p], row, onward[i],
        )

    def sum_wait(slot, p):
        ref = recv.at[slot, at_tiles(p)]
        remote(ref, ref, s4.at[0, p], r4.at[slot, p], row, c).wait_recv()

    def stage_a(u):
        take(u)
        for way in range(2):
            pass_copy(u, way).start()

    def stage_b(u):
        for way in range(2):
            pass_wait(u, way)
            forward_copy(u, way).start()

    def stage_c(u):
        for way in range(2):
            forward_wait(u, way)
        swap_copy(u).start()

    tb = row_tile(depth, 256)
    tm = row_tile(rows, 384)

    def stage_d(u):
        i, p = units[u]
        t0, n = pieces[p]
        q = blocks[i]
        cols = pl.ds(0, n * 128)
        swap_wait(u)

        @pl.loop(0, depth // tb)
        def _(t):
            at = pl.ds(pl.multiple_of(t * tb, tb), tb)
            for k in range(n):
                hi, lo = split(gath[q, t0 + k, at, :])
                b_hi[at, pl.ds(k * 128, 128)] = hi
                b_lo[at, pl.ds(k * 128, 128)] = lo

        @pl.loop(0, rows // tm)
        def _(t):
            at = pl.ds(pl.multiple_of(t * tm, tm), tm)
            dot = functools.partial(jnp.dot, preferred_element_type=jnp.float32)
            x = dot(a_hi[at, :], b_lo[:, cols]) + dot(a_lo[at, :], b_hi[:, cols])
            x = x + dot(a_hi[at, :], b_hi[:, cols])
            for k in range(n):
                part[i, t0 + k, at, :] = x[:, k * 128:(k + 1) * 128]

        if i < C - 1:
            @pl.when(m == 0)
            def _():
                if len(in_flight) == 2:
                    sum_copy(in_flight[0]).wait_send()
                sum_copy(u).start()

            if len(in_flight) == 2:
                in_flight.pop(0)
            in_flight.append(u)

    def add_in(i, slot, p):
        t0, n = pieces[p]

        @pl.loop(0, rows // ta)
        def _(t):
            at = pl.ds(pl.multiple_of(t * ta, ta), ta)
            for k in range(n):
                part[i, t0 + k, at, :] = part[i, t0 + k, at, :] + recv[slot, t0 + k, at, :]

    def stage_e(u):
        i, p = units[u]

        @pl.when(m == 1)
        def _():
            sum_wait(blocks[i], p)
            add_in(i, blocks[i], p)
            sum_copy(u).start()

    def gram_copy(n, p):
        to = lax.rem(row + n, R)
        return remote(
            gram.at[at_tiles(p), to], inbox.at[n - 1, at_tiles(p)],
            s5.at[n - 1, p], r5.at[n - 1, p], to, c,
        )

    def stage_f(p):
        t0, n = pieces[p]
        cols = pl.ds(0, n * 128)

        @pl.when(m == 1)
        def _():
            sum_wait(C, p)
            add_in(C - 1, C, p)

        sum_wait(c, p)

        @pl.loop(0, rows // ta)
        def _(t):
            at = pl.ds(pl.multiple_of(t * ta, ta), ta)
            for k in range(n):
                x = part[C - 1, t0 + k, at, :] + recv[c, t0 + k, at, :]
                out_ref[at, pl.ds((t0 + k) * 128, 128)] = -x * mask[t0 + k, at, :]
                hi, lo = split(x)
                b_hi[at, pl.ds(k * 128, 128)] = hi
                b_lo[at, pl.ds(k * 128, 128)] = lo

        dot = functools.partial(jnp.dot, preferred_element_type=jnp.float32)
        p_hi, p_lo = b_hi[pl.ds(0, rows), cols], b_lo[pl.ds(0, rows), cols]
        for r in range(0, R, 4):
            at = pl.ds(r * share, 4 * share)
            x = dot(t_hi[at, :], p_lo) + dot(t_lo[at, :], p_hi) + dot(t_hi[at, :], p_hi)
            for e in range(4):
                for k in range(n):
                    gram[t0 + k, r + e] = x[e * share:(e + 1) * share, k * 128:(k + 1) * 128]
        for k in range(1, R):
            gram_copy(k, p).start()

    def stage_g(p):
        t0, n = pieces[p]
        for k in range(1, R):
            gram_copy(k, p).wait_recv()
        for k in range(n):
            t = t0 + k
            x = gram[t, row]
            for d in range(R - 1):
                x = x + inbox[d, t]
            at = pl.ds(t * 128, 128)
            r = lax.broadcasted_iota(jnp.int32, (share, 128), 0) + row * share
            q = lax.broadcasted_iota(jnp.int32, (share, 128), 1) + t * 128
            inside = (r < width) & (q < width)
            dout_ref[:, at] = jnp.where(inside, diag_ref[:, at] + x, 0.0)

    total = len(units)
    finished = 0
    in_flight = []

    def due(u, lag):
        wait = 1 if u >= C else 0
        return u + lag + wait

    for step in range(due(total, 7)):
        for u in range(total):
            i, p = units[u]
            if due(u, 7) == step:
                if i < C - 1:
                    stage_e(u)
                if p and i == (0 if p == len(pieces) - 1 else C - 2):
                    stage_f(p - 1)
                    finished = p
        for lag, stage in ((3, stage_d), (2, stage_c), (1, stage_b), (0, stage_a)):
            for u in range(total):
                if due(u, lag) == step:
                    stage(u)
    for p in range(finished, len(pieces)):
        stage_f(p)
    for p in range(len(pieces)):
        stage_g(p)

    for p in range(len(pieces)):
        line_sent(p)
        for d in range(1, C):
            spread_copy(d, p).wait_send()
        for k in range(1, R):
            gram_copy(k, p).wait_send()
    for u in range(total):
        for way in range(2):
            pass_copy(u, way).wait_send()
            forward_copy(u, way).wait_send()
        swap_copy(u).wait_send()

    @pl.when(m == 0)
    def _():
        for u in in_flight:
            sum_copy(u).wait_send()

    @pl.when(m == 1)
    def _():
        for u in range(total):
            if units[u][0] < C - 1:
                sum_copy(u).wait_send()


def line_product(R, C, a, f, diag, widths, member):
    rows, depth = a.shape
    cols = f.shape[1]
    tiles = cols // 128
    pieces = len(pieces_of(tiles))
    units = C * pieces
    f32, bf16 = jnp.float32, jnp.bfloat16
    vmem = pl.BlockSpec(memory_space=pltpu.VMEM)
    smem = pl.BlockSpec(memory_space=pltpu.SMEM)
    hbm = pl.BlockSpec(memory_space=pl.ANY)
    dma = pltpu.SemaphoreType.DMA
    return pl.pallas_call(
        functools.partial(line_kernel, R, C),
        out_shape=[
            pltpu.VMEM((rows, cols), f32),
            pltpu.VMEM((W // R, cols), f32),
        ],
        in_specs=[hbm, hbm, vmem, smem, vmem],
        out_specs=[vmem, vmem],
        scratch_shapes=[
            pltpu.VMEM((rows, depth), f32),
            pltpu.VMEM((tiles, rows, 128), f32),
            pltpu.VMEM((tiles, rows, 128), f32),
            pltpu.VMEM((C - 1, tiles, rows // C, 128), f32),
            pltpu.VMEM((C, tiles, depth, 128), f32),
            pltpu.VMEM((C, tiles, rows, 128), f32),
            pltpu.VMEM((C + 1, tiles, rows, 128), f32),
            pltpu.VMEM((rows, depth), bf16),
            pltpu.VMEM((rows, depth), bf16),
            pltpu.VMEM((depth, 256), bf16),
            pltpu.VMEM((depth, 256), bf16),
            pltpu.VMEM((W, rows), bf16),
            pltpu.VMEM((W, rows), bf16),
            pltpu.VMEM((tiles, R, W // R, 128), f32),
            pltpu.VMEM((R - 1, tiles, W // R, 128), f32),
            dma((tiles + 1,)),
            dma((pieces,)),
            dma((C - 1, pieces)),
            dma((C - 1, pieces)),
            dma((units, 2)),
            dma((units, 2)),
            dma((units, 2)),
            dma((units, 2)),
            dma((units,)),
            dma((units,)),
            dma((C - 1, pieces)),
            dma((C + 1, pieces)),
            dma((R - 1, pieces)),
            dma((R - 1, pieces)),
            dma((C, pieces)),
            dma((C, pieces)),
        ],
        compiler_params=pltpu.CompilerParams(
            collective_id=1, has_side_effects=True, vmem_limit_bytes=64000000
        ),
    )(a, f, diag, widths, member)


def per_device(ancestor_inverse, factor, diag_inverse, widths, member):
    R = lax.axis_size("row")
    C = lax.axis_size("col")
    my_row = lax.axis_index("row")
    my_col = lax.axis_index("col")
    shard_cols = factor.shape[1]
    rows, depth = ancestor_inverse.shape
    if C == NODES and R == 2 * C and shard_cols == W and depth == 2 * rows:
        return tuple(line_product(R, C, ancestor_inverse, factor, diag_inverse, widths, member))
    col_start = my_col * shard_cols
    global_cols = col_start + jnp.arange(shard_cols, dtype=jnp.int32)
    node_of = global_cols // W
    within = global_cols % W
    select = node_of[None, :] == jnp.arange(NODES, dtype=jnp.int32)[:, None]
    width_col = jnp.sum(jnp.where(select, widths[:, None], 0), axis=0)
    col_keep = within < width_col
    pick = jnp.where(select & col_keep[None, :], 1.0, 0.0).astype(jnp.bfloat16)
    mask = lax.dot_general(
        member.astype(jnp.bfloat16), pick, (((0,), (0,)), ((), ())),
        preferred_element_type=jnp.float32,
    )
    masked = factor * mask
    if shard_cols == W:
        left = masked
    else:
        rows_full = lax.all_gather(masked, "col", axis=1, tiled=True)
        left = lax.dynamic_slice_in_dim(rows_full, col_start // W * W, W, 1)
    product, gram = grid_product(R, C, ancestor_inverse, masked, left)
    offdiag = -product * mask
    diag_rows = diag_inverse.shape[0]
    local_rows = my_row * diag_rows + jnp.arange(diag_rows, dtype=jnp.int32)
    inside = (local_rows[:, None] < width_col[None, :]) & col_keep[None, :]
    diag_blocks = (diag_inverse + gram) * inside.astype(jnp.float32)
    return (offdiag, diag_blocks)


def solution(mesh):
    in_specs = (P("row", "col"), P("row", "col"), P("row", "col"), P(), P(None, "row"))
    out_specs = (P("row", "col"), P("row", "col"))
    return jax.shard_map(
        per_device, mesh=mesh, in_specs=in_specs, out_specs=out_specs, check_vma=False
    )
```

```python
import functools

import jax
import jax.numpy as jnp
from jax import lax
from jax.experimental import pallas as pl
from jax.experimental.pallas import tpu as pltpu
from jax.sharding import PartitionSpec as P

W = 640
NODES = 4
MESH = pl.DeviceIdType.MESH


def split(x):
    hi = x.astype(jnp.bfloat16)
    lo = (x - hi.astype(jnp.float32)).astype(jnp.bfloat16)
    return hi, lo


def row_tile(rows, most):
    return max(t for t in range(16, most + 1, 16) if rows % t == 0)


def product_kernel(
    R, C, a_ref, l_ref, left_ref, out_ref, gram_ref, mid, gath, part, recv, gram, inbox,
    a_hi, a_lo, b_hi, b_lo, s0, r0, s1, r1, s2, r2, s3, r3, s4, r4, s5, r5, own_sem,
):
    G = R // C
    half_ring = C // 2
    row = lax.axis_index("row")
    c = lax.axis_index("col")
    j = row // G
    g = lax.rem(row, G)
    rows, cols = l_ref.shape
    depth = a_ref.shape[1]
    chunk = rows // C
    half = rows // 2

    barrier = pltpu.get_barrier_semaphore()

    def greet(r, q):
        pl.semaphore_signal(barrier, inc=1, device_id=(r, q), device_id_type=MESH)

    for m in range(1, R):
        greet(lax.rem(row + m, R), c)
    for m in range(1, C):
        greet(row, lax.rem(c + m, C))
    pl.semaphore_wait(barrier, R + C - 2)

    def remote(src, dst, ssem, rsem, r, q):
        return pltpu.make_async_remote_copy(
            src_ref=src, dst_ref=dst, send_sem=ssem, recv_sem=rsem,
            device_id=(r, q), device_id_type=MESH,
        )

    mine = pl.ds(pl.multiple_of(j * chunk, chunk), chunk)

    def spread_copy(m):
        n = lax.rem(j + m, C)
        src = l_ref.at[pl.ds(pl.multiple_of(n * chunk, chunk), chunk)]
        return remote(src, mid.at[j], s0.at[m - 1], r0.at[m - 1], n * G + g, c)

    def column_copy(p, m):
        return remote(
            mid.at[p], gath.at[c, g, mine], s1.at[m - 1], r1.at[m - 1], row, p
        )

    for m in range(1, C):
        spread_copy(m).start()
    own = pltpu.make_async_copy(l_ref.at[mine], mid.at[j], own_sem.at[0])
    own.start()
    own.wait()
    for m in range(1, C):
        ref = mid.at[lax.rem(j + C - m, C)]
        remote(ref, ref, s0.at[m - 1], r0.at[m - 1], row, c).wait_recv()
    ways_on = sorted(range(1, C), key=lambda m: -min(m, C - m))
    for m in ways_on:
        column_copy(lax.rem(c + m, C), m).start()
    keep = pltpu.make_async_copy(mid.at[c], gath.at[c, g, mine], own_sem.at[1])
    keep.start()

    ta = row_tile(rows, 128)

    @pl.loop(0, rows // ta)
    def _(t):
        at = pl.ds(pl.multiple_of(t * ta, ta), ta)
        hi, lo = split(a_ref[at, :])
        a_hi[at, pl.ds(0, depth)] = hi
        a_lo[at, pl.ds(0, depth)] = lo

    order = [(0, 0), (half_ring, 0)]
    for s in range(half_ring - 1, 0, -1):
        order += [(s, -1), (s, 1)]
    blocks = []
    for s, way in order:
        blocks.append(lax.rem(c + (s if way >= 0 else C - s), C))

    def plane_copy(i, m):
        ref = gath.at[blocks[i], g, mine]
        return remote(ref, ref, s2.at[i, m - 1], r2.at[i, m - 1], lax.rem(j + m, C) * G + g, c)

    def plane_wait(i, m):
        from_j = lax.rem(j + C - m, C)
        ref = gath.at[blocks[i], g, pl.ds(pl.multiple_of(from_j * chunk, chunk), chunk)]
        remote(ref, ref, s2.at[i, m - 1], r2.at[i, m - 1], row, c).wait_recv()

    def group_copy(i, n):
        ref = gath.at[blocks[i], g]
        return remote(ref, ref, s3.at[i, n - 1], r3.at[i, n - 1], j * G + lax.rem(g + n, G), c)

    def group_wait(i, n):
        ref = gath.at[blocks[i], lax.rem(g + G - n, G)]
        remote(ref, ref, s3.at[i, n - 1], r3.at[i, n - 1], row, c).wait_recv()

    for i, (s, way) in enumerate(order):
        if s:
            m = C - s if way >= 0 else s
            ref = gath.at[blocks[i], g, mine]
            remote(ref, ref, s1.at[m - 1], r1.at[m - 1], row, c).wait_recv()
        else:
            keep.wait()
        for m in range(1, C):
            plane_copy(i, m).start()

    tb = row_tile(rows, 128)
    tm = row_tile(rows, 256)

    def multiply(i):
        q = blocks[i]
        for gg in range(G):
            @pl.loop(0, rows // tb)
            def _(t):
                hi, lo = split(gath[q, gg, pl.ds(pl.multiple_of(t * tb, tb), tb), :])
                at = pl.ds(pl.multiple_of(gg * rows + t * tb, tb), tb)
                b_hi[at, :] = hi
                b_lo[at, :] = lo

        @pl.loop(0, rows // tm)
        def _(t):
            at = pl.ds(pl.multiple_of(t * tm, tm), tm)
            dot = functools.partial(jnp.dot, preferred_element_type=jnp.float32)
            x_hi, x_lo = a_hi[at, pl.ds(0, depth)], a_lo[at, pl.ds(0, depth)]
            y_hi, y_lo = b_hi[pl.ds(0, depth), :], b_lo[pl.ds(0, depth), :]
            part[i, at, :] = dot(x_hi, y_lo) + dot(x_lo, y_hi) + dot(x_hi, y_hi)

    def ring_copy(i, way, s):
        to = lax.rem(c + (C - 1 if way == 0 else 1), C)
        piece = pl.ds(way * half, half) if s == half_ring else pl.ds(0, rows)
        return remote(
            part.at[i, piece], recv.at[way, s - 1, piece],
            s4.at[way, s - 1], r4.at[way, s - 1], row, to,
        )

    def ring_wait(way, s):
        piece = pl.ds(way * half, half) if s + 1 == half_ring else pl.ds(0, rows)
        ref = recv.at[way, s, piece]
        remote(ref, ref, s4.at[way, s], r4.at[way, s], row, c).wait_recv()

    def accumulate(i, way, s):
        lo, n = (way * half, half) if s + 1 == half_ring else (0, rows)
        step = row_tile(n, 128)

        @pl.loop(0, n // step)
        def _(t):
            at = pl.ds(pl.multiple_of(lo + t * step, 16), step)
            part[i, at, :] = part[i, at, :] + recv[way, s, at, :]

    sends = []
    for i, (s, way) in enumerate(order):
        for m in range(1, C):
            plane_wait(i, m)
        for n in range(1, G):
            group_copy(i, n).start()
        for n in range(1, G):
            group_wait(i, n)
        multiply(i)
        if s == half_ring:
            ways = (0, 1)
        elif s:
            ways = (0,) if way < 0 else (1,)
        else:
            ways = ()
        for w in ways:
            if s < half_ring:
                ring_wait(w, s)
                accumulate(i, w, s)
            copy = ring_copy(i, w, s)
            copy.start()
            sends.append(copy)

    ring_wait(0, 0)
    ring_wait(1, 0)

    @pl.loop(0, rows // ta)
    def _(t):
        at = pl.ds(pl.multiple_of(t * ta, ta), ta)
        x = part[0, at, :] + recv[0, 0, at, :] + recv[1, 0, at, :]
        out_ref[at, :] = x
        hi, lo = split(x)
        b_hi[at, :] = hi
        b_lo[at, :] = lo
        hi, lo = split(left_ref[at, :])
        a_hi[at, pl.ds(0, W)] = hi
        a_lo[at, pl.ds(0, W)] = lo

    for t in range(W // 128):
        at = pl.ds(t * 128, 128)
        dot = functools.partial(
            lax.dot_general, dimension_numbers=(((0,), (0,)), ((), ())),
            preferred_element_type=jnp.float32,
        )
        p_hi, p_lo = b_hi[pl.ds(0, rows), :], b_lo[pl.ds(0, rows), :]
        x = dot(a_hi[:, at], p_lo) + dot(a_lo[:, at], p_hi)
        gram[at, :] = x + dot(a_hi[:, at], p_hi)

    share = W // R

    def gram_copy(m):
        to = lax.rem(row + m, R)
        src = gram.at[pl.ds(pl.multiple_of(to * share, 8), share)]
        return remote(src, inbox.at[m - 1], s5.at[m - 1], r5.at[m - 1], to, c)

    for m in range(1, R):
        gram_copy(m).start()
    total = gram[pl.ds(pl.multiple_of(row * share, 8), share), :]
    for m in range(1, R):
        gram_copy(m).wait_recv()
        total = total + inbox[m - 1]
    gram_ref[...] = total

    for copy in sends:
        copy.wait_send()
    for m in range(1, C):
        spread_copy(m).wait_send()
        column_copy(lax.rem(c + m, C), m).wait_send()
    for m in range(1, R):
        gram_copy(m).wait_send()
    for i in range(C):
        for m in range(1, C):
            plane_copy(i, m).wait_send()
        for n in range(1, G):
            group_copy(i, n).wait_send()


def grid_product(R, C, a, l, left):
    rows, cols = l.shape
    G = R // C
    depth = a.shape[1]
    vmem = pl.BlockSpec(memory_space=pltpu.VMEM)
    dma = pltpu.SemaphoreType.DMA
    return pl.pallas_call(
        functools.partial(product_kernel, R, C),
        out_shape=[
            jax.ShapeDtypeStruct((rows, cols), jnp.float32),
            jax.ShapeDtypeStruct((W // R, cols), jnp.float32),
        ],
        in_specs=[vmem, vmem, vmem],
        out_specs=[vmem, vmem],
        scratch_shapes=[
            pltpu.VMEM((C, rows // C, cols), jnp.float32),
            pltpu.VMEM((C, G, rows, cols), jnp.float32),
            pltpu.VMEM((C, rows, cols), jnp.float32),
            pltpu.VMEM((2, C // 2, rows, cols), jnp.float32),
            pltpu.VMEM((W, cols), jnp.float32),
            pltpu.VMEM((R - 1, W // R, cols), jnp.float32),
            pltpu.VMEM((rows, max(depth, W)), jnp.bfloat16),
            pltpu.VMEM((rows, max(depth, W)), jnp.bfloat16),
            pltpu.VMEM((max(depth, rows), cols), jnp.bfloat16),
            pltpu.VMEM((max(depth, rows), cols), jnp.bfloat16),
            dma((C - 1,)),
            dma((C - 1,)),
            dma((C - 1,)),
            dma((C - 1,)),
            dma((C, C - 1)),
            dma((C, C - 1)),
            dma((C, max(G - 1, 1))),
            dma((C, max(G - 1, 1))),
            dma((2, C // 2)),
            dma((2, C // 2)),
            dma((R - 1,)),
            dma((R - 1,)),
            dma((2,)),
        ],
        compiler_params=pltpu.CompilerParams(
            collective_id=0, has_side_effects=True, vmem_limit_bytes=67043328
        ),
    )(a, l, left)


CUTS = 2


def pieces_of(tiles):
    sizes = [1]
    while sum(sizes) < tiles:
        sizes.append(2 if tiles - sum(sizes) > 2 else 1)
    return [(sum(sizes[:p]), n) for p, n in enumerate(sizes)]


def line_kernel(
    R, C, a_hbm, f_hbm, diag_ref, widths_ref, member_ref, out_ref, dout_ref,
    a_raw, mask, lm, mid, gath, part, recv, a_hi, a_lo, b_hi, b_lo, t_hi, t_lo,
    gram, inbox, in_sem, own_sem, s0, r0, s1, r1, s2, r2, s3, r3, s4, r4, s5, r5, s6, r6,
):
    rows, depth = a_raw.shape
    tiles = lm.shape[0]
    G = R // C
    chunk = rows // C
    half = chunk // 2
    share = W // R
    pieces = pieces_of(tiles)
    row = lax.axis_index("row")
    c = lax.axis_index("col")
    j = row // G
    g = lax.rem(row, G)
    other = 1 - g
    jx = j + 1 - 2 * lax.rem(j, 2)
    jy = lax.rem(j + 2, C)
    jd = C - 1 - j
    last = C - 1
    h = c // 2
    m = c + h * (last - 2 * c)

    def flip(n):
        return n + h * (last - 2 * n)

    blocks = [flip(3), flip(2 - 2 * m), flip(1 + m), c]
    onward = [flip(m + 1), flip(1 - m), flip(m + 1)]
    slots = [blocks[0], blocks[1], blocks[2] + m * (C - blocks[2])]

    def load_f(t):
        return pltpu.make_async_copy(f_hbm.at[:, pl.ds(t * 128, 128)], lm.at[t], in_sem.at[t])

    load_a = pltpu.make_async_copy(a_hbm, a_raw, in_sem.at[tiles])
    for t in range(tiles):
        load_f(t).start()
    load_a.start()

    barrier = pltpu.get_barrier_semaphore()

    def greet(r, q):
        pl.semaphore_signal(barrier, inc=1, device_id=(r, q), device_id_type=MESH)

    for n in range(1, R):
        greet(lax.rem(row + n, R), c)

    for n in range(1, C):
        greet(row, lax.rem(c + n, C))

    keep = lax.broadcasted_iota(jnp.int32, (NODES, 128), 0) == c
    width = widths_ref[c]
    member = member_ref[...].astype(jnp.float32).astype(jnp.bfloat16)

    def make_mask(t):
        q = lax.broadcasted_iota(jnp.int32, (NODES, 128), 1) + t * 128
        pick = jnp.where(keep & (q < width), 1.0, 0.0).astype(jnp.bfloat16)
        x = lax.dot_general(
            member, pick, (((0,), (0,)), ((), ())), preferred_element_type=jnp.float32
        )
        load_f(t).wait()
        mask[t] = x
        lm[t] = lm[t] * x

    for t in range(pieces[0][1]):
        make_mask(t)

    pl.semaphore_wait(barrier, R + C - 2)

    def remote(src, dst, ssem, rsem, r, q):
        return pltpu.make_async_remote_copy(
            src_ref=src, dst_ref=dst, send_sem=ssem, recv_sem=rsem,
            device_id=(r, q), device_id_type=MESH,
        )

    def at_tiles(p):
        t, n = pieces[p]
        return pl.ds(t, n)

    def spot(gg, jj, n=None, k=0):
        start = gg * rows + jj * chunk + k * half
        return pl.ds(pl.multiple_of(start, 8), half if n else chunk)

    mine = pl.ds(pl.multiple_of(j * chunk, 8), chunk)
    near = [j, jx, jy, jd]

    def spread_copy(d, p):
        src = lm.at[at_tiles(p), pl.ds(pl.multiple_of(near[d] * chunk, 8), chunk)]
        dst = mid.at[d - 1, at_tiles(p)]
        return remote(src, dst, s0.at[d - 1, p], r0.at[d - 1, p], near[d] * G + g, c)

    def spread_start(p, ways=(1, 2, 3)):
        for d in ways:
            spread_copy(d, p).start()

    def line_source(d, p):
        return mid.at[d - 1, at_tiles(p)] if d else lm.at[at_tiles(p), mine]

    def line_copy(d, p):
        dst = gath.at[c, at_tiles(p), spot(g, j)]
        return remote(line_source(d, p), dst, s6.at[d, p], r6.at[c, p], row, near[d])

    def keep_copy(d, p):
        dst = gath.at[c, at_tiles(p), spot(g, j)]
        return pltpu.make_async_copy(line_source(d, p), dst, own_sem.at[p])

    def line_start(d, p):
        if d:
            spread_copy(d, p).wait_recv()

        @pl.when(near[d] != c)
        def _():
            line_copy(d, p).start()

        @pl.when(near[d] == c)
        def _():
            keep_copy(d, p).start()

    def line_sent(p):
        for d in range(C):
            @pl.when(near[d] != c)
            def _():
                line_copy(d, p).wait_send()

    spread_start(0, (1, 2, 3))
    line_start(0, 0)
    for t in range(pieces[0][1], tiles):
        make_mask(t)
    spread_start(1, (1, 2, 3))
    for d in range(1, C):
        line_start(d, 0)
    for p in range(2, len(pieces)):
        spread_start(p)
    for p in range(1, len(pieces)):
        line_start(0, p)
    load_a.wait()
    ta = row_tile(rows, 128)

    @pl.loop(0, rows // ta)
    def _(t):
        at = pl.ds(pl.multiple_of(t * ta, ta), ta)
        hi, lo = split(a_raw[at, :])
        a_hi[at, :] = hi
        a_lo[at, :] = lo

    for t in range(tiles):
        hi, lo = split(lm[t].T)
        t_hi[pl.ds(t * 128, 128), :] = hi
        t_lo[pl.ds(t * 128, 128), :] = lo

    for p in range(1, len(pieces)):
        for d in range(1, C):
            line_start(d, p)
    units = [(i, p) for p in range(len(pieces)) for i in range(C)]

    def take(u):
        i, p = units[u]
        if i == C - 1:
            keep_copy(0, p).wait()
        else:
            ref = gath.at[blocks[i], at_tiles(p), spot(g, j)]
            remote(ref, ref, s6.at[0, p], r6.at[blocks[i], p], row, c).wait_recv()

    def pass_copy(u, way):
        i, p = units[u]
        ref = gath.at[blocks[i], at_tiles(p), spot(g, j)]
        to = jx if way == 0 else jy
        return remote(ref, ref, s1.at[u, way], r1.at[u, way], to * G + g, c)

    def pass_wait(u, way):
        i, p = units[u]
        ref = gath.at[blocks[i], at_tiles(p), spot(g, jx if way == 0 else jy)]
        remote(ref, ref, s1.at[u, way], r1.at[u, way], row, c).wait_recv()

    def forward_copy(u, way):
        i, p = units[u]
        ref = gath.at[blocks[i], at_tiles(p), spot(g, jx if way == 0 else jy, 1, way)]
        to = jy if way == 0 else jx
        return remote(ref, ref, s2.at[u, way], r2.at[u, way], to * G + g, c)

    def forward_wait(u, way):
        i, p = units[u]
        ref = gath.at[blocks[i], at_tiles(p), spot(g, jd, 1, way)]
        remote(ref, ref, s2.at[u, way], r2.at[u, way], row, c).wait_recv()

    def swap_copy(u):
        i, p = units[u]
        ref = gath.at[blocks[i], at_tiles(p), pl.ds(pl.multiple_of(g * rows, 8), rows)]
        return remote(ref, ref, s3.at[u], r3.at[u], j * G + other, c)

    def swap_wait(u):
        i, p = units[u]
        ref = gath.at[blocks[i], at_tiles(p), pl.ds(pl.multiple_of(other * rows, 8), rows)]
        remote(ref, ref, s3.at[u], r3.at[u], row, c).wait_recv()

    def bands(p):
        n = CUTS if p == len(pieces) - 1 else 1
        return [(p + k, k * (rows // n), rows // n) for k in range(n)]

    def sum_copy(u, band):
        i, p = units[u]
        sem, lo, n = band
        at = pl.ds(lo, n)
        return remote(
            part.at[i, at_tiles(p), at], recv.at[slots[i], at_tiles(p), at],
            s4.at[i, sem], r4.at[slots[i], sem], row, onward[i],
        )

    def sum_sent(u):
        for band in bands(units[u][1]):
            sum_copy(u, band).wait_send()

    def sum_wait(slot, p, band):
        sem, lo, n = band
        ref = recv.at[slot, at_tiles(p), pl.ds(lo, n)]
        remote(ref, ref, s4.at[0, sem], r4.at[slot, sem], row, c).wait_recv()

    def stage_a(u):
        take(u)
        for way in range(2):
            pass_copy(u, way).start()

    def stage_b(u):
        for way in range(2):
            pass_wait(u, way)
            forward_copy(u, way).start()

    def stage_c(u):
        for way in range(2):
            forward_wait(u, way)
        swap_copy(u).start()

    tb = row_tile(depth, 256)
    tm = row_tile(rows, 384)

    def stage_d(u):
        i, p = units[u]
        t0, n = pieces[p]
        q = blocks[i]
        cols = pl.ds(0, n * 128)
        swap_wait(u)

        @pl.loop(0, depth // tb)
        def _(t):
            at = pl.ds(pl.multiple_of(t * tb, tb), tb)
            for k in range(n):
                hi, lo = split(gath[q, t0 + k, at, :])
                b_hi[at, pl.ds(k * 128, 128)] = hi
                b_lo[at, pl.ds(k * 128, 128)] = lo

        @pl.loop(0, rows // tm)
        def _(t):
            at = pl.ds(pl.multiple_of(t * tm, tm), tm)
            dot = functools.partial(jnp.dot, preferred_element_type=jnp.float32)
            x = dot(a_hi[at, :], b_lo[:, cols]) + dot(a_lo[at, :], b_hi[:, cols])
            x = x + dot(a_hi[at, :], b_hi[:, cols])
            for k in range(n):
                part[i, t0 + k, at, :] = x[:, k * 128:(k + 1) * 128]

        if i < C - 1:
            @pl.when(m == 0)
            def _():
                if len(in_flight) == 2:
                    sum_sent(in_flight[0])
                for band in bands(p):
                    sum_copy(u, band).start()

            if len(in_flight) == 2:
                in_flight.pop(0)
            in_flight.append(u)

    def add_in(i, slot, p, band):
        t0, n = pieces[p]
        sem, lo, many = band
        step = row_tile(many, 128)

        @pl.loop(0, many // step)
        def _(t):
            at = pl.ds(pl.multiple_of(lo + t * step, 16), step)
            for k in range(n):
                part[i, t0 + k, at, :] = part[i, t0 + k, at, :] + recv[slot, t0 + k, at, :]

    def stage_e(u):
        i, p = units[u]

        @pl.when(m == 1)
        def _():
            for band in bands(p):
                sum_wait(blocks[i], p, band)
                add_in(i, blocks[i], p, band)
                sum_copy(u, band).start()

    def gram_copy(n, p):
        to = lax.rem(row + n, R)
        return remote(
            gram.at[at_tiles(p), to], inbox.at[n - 1, at_tiles(p)],
            s5.at[n - 1, p], r5.at[n - 1, p], to, c,
        )

    def stage_f(p):
        t0, n = pieces[p]
        cols = pl.ds(0, n * 128)

        @pl.when(m == 1)
        def _():
            for band in bands(p):
                sum_wait(C, p, band)
                add_in(C - 1, C, p, band)

        def finish(band):
            sum_wait(c, p, band)
            sem, lo, many = band
            step = row_tile(many, 128)

            @pl.loop(0, many // step)
            def _(t):
                at = pl.ds(pl.multiple_of(lo + t * step, 16), step)
                for k in range(n):
                    x = part[C - 1, t0 + k, at, :] + recv[c, t0 + k, at, :]
                    out_ref[at, pl.ds((t0 + k) * 128, 128)] = -x * mask[t0 + k, at, :]
                    hi, lo_part = split(x)
                    b_hi[at, pl.ds(k * 128, 128)] = hi
                    b_lo[at, pl.ds(k * 128, 128)] = lo_part

        for band in bands(p):
            finish(band)

        dot = functools.partial(jnp.dot, preferred_element_type=jnp.float32)
        p_hi, p_lo = b_hi[pl.ds(0, rows), cols], b_lo[pl.ds(0, rows), cols]
        for r in range(0, R, 4):
            at = pl.ds(r * share, 4 * share)
            x = dot(t_hi[at, :], p_lo) + dot(t_lo[at, :], p_hi) + dot(t_hi[at, :], p_hi)
            for e in range(4):
                for k in range(n):
                    gram[t0 + k, r + e] = x[e * share:(e + 1) * share, k * 128:(k + 1) * 128]
        for k in range(1, R):
            gram_copy(k, p).start()

    def stage_g(p):
        t0, n = pieces[p]
        for k in range(1, R):
            gram_copy(k, p).wait_recv()
        for k in range(n):
            t = t0 + k
            x = gram[t, row]
            for d in range(R - 1):
                x = x + inbox[d, t]
            at = pl.ds(t * 128, 128)
            r = lax.broadcasted_iota(jnp.int32, (share, 128), 0) + row * share
            q = lax.broadcasted_iota(jnp.int32, (share, 128), 1) + t * 128
            inside = (r < width) & (q < width)
            dout_ref[:, at] = jnp.where(inside, diag_ref[:, at] + x, 0.0)

    total = len(units)
    finished = 0
    in_flight = []

    def due(u, lag):
        wait = 1 if u >= C else 0
        return u + lag + wait

    for step in range(due(total, 7)):
        for u in range(total):
            i, p = units[u]
            if due(u, 7) == step:
                if i < C - 1:
                    stage_e(u)
                if p and i == (0 if p == len(pieces) - 1 else C - 2):
                    stage_f(p - 1)
                    finished = p
        for lag, stage in ((3, stage_d), (2, stage_c), (1, stage_b), (0, stage_a)):
            for u in range(total):
                if due(u, lag) == step:
                    stage(u)
    for p in range(finished, len(pieces)):
        stage_f(p)
    for p in range(len(pieces)):
        stage_g(p)

    for p in range(len(pieces)):
        line_sent(p)
        for d in range(1, C):
            spread_copy(d, p).wait_send()
        for k in range(1, R):
            gram_copy(k, p).wait_send()
    for u in range(total):
        for way in range(2):
            pass_copy(u, way).wait_send()
            forward_copy(u, way).wait_send()
        swap_copy(u).wait_send()

    @pl.when(m == 0)
    def _():
        for u in in_flight:
            sum_sent(u)

    @pl.when(m == 1)
    def _():
        for u in range(total):
            if units[u][0] < C - 1:
                sum_sent(u)


def line_product(R, C, a, f, diag, widths, member):
    rows, depth = a.shape
    cols = f.shape[1]
    tiles = cols // 128
    pieces = len(pieces_of(tiles))
    units = C * pieces
    f32, bf16 = jnp.float32, jnp.bfloat16
    vmem = pl.BlockSpec(memory_space=pltpu.VMEM)
    smem = pl.BlockSpec(memory_space=pltpu.SMEM)
    hbm = pl.BlockSpec(memory_space=pl.ANY)
    dma = pltpu.SemaphoreType.DMA
    return pl.pallas_call(
        functools.partial(line_kernel, R, C),
        out_shape=[
            pltpu.VMEM((rows, cols), f32),
            pltpu.VMEM((W // R, cols), f32),
        ],
        in_specs=[hbm, hbm, vmem, smem, vmem],
        out_specs=[vmem, vmem],
        scratch_shapes=[
            pltpu.VMEM((rows, depth), f32),
            pltpu.VMEM((tiles, rows, 128), f32),
            pltpu.VMEM((tiles, rows, 128), f32),
            pltpu.VMEM((C - 1, tiles, rows // C, 128), f32),
            pltpu.VMEM((C, tiles, depth, 128), f32),
            pltpu.VMEM((C, tiles, rows, 128), f32),
            pltpu.VMEM((C + 1, tiles, rows, 128), f32),
            pltpu.VMEM((rows, depth), bf16),
            pltpu.VMEM((rows, depth), bf16),
            pltpu.VMEM((depth, 256), bf16),
            pltpu.VMEM((depth, 256), bf16),
            pltpu.VMEM((W, rows), bf16),
            pltpu.VMEM((W, rows), bf16),
            pltpu.VMEM((tiles, R, W // R, 128), f32),
            pltpu.VMEM((R - 1, tiles, W // R, 128), f32),
            dma((tiles + 1,)),
            dma((pieces,)),
            dma((C - 1, pieces)),
            dma((C - 1, pieces)),
            dma((units, 2)),
            dma((units, 2)),
            dma((units, 2)),
            dma((units, 2)),
            dma((units,)),
            dma((units,)),
            dma((C - 1, pieces + CUTS - 1)),
            dma((C + 1, pieces + CUTS - 1)),
            dma((R - 1, pieces)),
            dma((R - 1, pieces)),
            dma((C, pieces)),
            dma((C, pieces)),
        ],
        compiler_params=pltpu.CompilerParams(
            collective_id=1, has_side_effects=True, vmem_limit_bytes=64000000
        ),
    )(a, f, diag, widths, member)


def per_device(ancestor_inverse, factor, diag_inverse, widths, member):
    R = lax.axis_size("row")
    C = lax.axis_size("col")
    my_row = lax.axis_index("row")
    my_col = lax.axis_index("col")
    shard_cols = factor.shape[1]
    rows, depth = ancestor_inverse.shape
    if C == NODES and R == 2 * C and shard_cols == W and depth == 2 * rows:
        return tuple(line_product(R, C, ancestor_inverse, factor, diag_inverse, widths, member))
    col_start = my_col * shard_cols
    global_cols = col_start + jnp.arange(shard_cols, dtype=jnp.int32)
    node_of = global_cols // W
    within = global_cols % W
    select = node_of[None, :] == jnp.arange(NODES, dtype=jnp.int32)[:, None]
    width_col = jnp.sum(jnp.where(select, widths[:, None], 0), axis=0)
    col_keep = within < width_col
    pick = jnp.where(select & col_keep[None, :], 1.0, 0.0).astype(jnp.bfloat16)
    mask = lax.dot_general(
        member.astype(jnp.bfloat16), pick, (((0,), (0,)), ((), ())),
        preferred_element_type=jnp.float32,
    )
    masked = factor * mask
    if shard_cols == W:
        left = masked
    else:
        rows_full = lax.all_gather(masked, "col", axis=1, tiled=True)
        left = lax.dynamic_slice_in_dim(rows_full, col_start // W * W, W, 1)
    product, gram = grid_product(R, C, ancestor_inverse, masked, left)
    offdiag = -product * mask
    diag_rows = diag_inverse.shape[0]
    local_rows = my_row * diag_rows + jnp.arange(diag_rows, dtype=jnp.int32)
    inside = (local_rows[:, None] < width_col[None, :]) & col_keep[None, :]
    diag_blocks = (diag_inverse + gram) * inside.astype(jnp.float32)
    return (offdiag, diag_blocks)


def solution(mesh):
    in_specs = (P("row", "col"), P("row", "col"), P("row", "col"), P(), P(None, "row"))
    out_specs = (P("row", "col"), P("row", "col"))
    return jax.shard_map(
        per_device, mesh=mesh, in_specs=in_specs, out_specs=out_specs, check_vma=False
    )
```

```python
import functools

import jax
import jax.numpy as jnp
from jax import lax
from jax.experimental import pallas as pl
from jax.experimental.pallas import tpu as pltpu
from jax.sharding import PartitionSpec as P

W = 640
NODES = 4
MESH = pl.DeviceIdType.MESH


def split(x):
    hi = x.astype(jnp.bfloat16)
    lo = (x - hi.astype(jnp.float32)).astype(jnp.bfloat16)
    return hi, lo


def row_tile(rows, most):
    return max(t for t in range(16, most + 1, 16) if rows % t == 0)


def product_kernel(
    R, C, a_ref, l_ref, left_ref, out_ref, gram_ref, mid, gath, part, recv, gram, inbox,
    a_hi, a_lo, b_hi, b_lo, s0, r0, s1, r1, s2, r2, s3, r3, s4, r4, s5, r5, own_sem,
):
    G = R // C
    half_ring = C // 2
    row = lax.axis_index("row")
    c = lax.axis_index("col")
    j = row // G
    g = lax.rem(row, G)
    rows, cols = l_ref.shape
    depth = a_ref.shape[1]
    chunk = rows // C
    half = rows // 2

    barrier = pltpu.get_barrier_semaphore()

    def greet(r, q):
        pl.semaphore_signal(barrier, inc=1, device_id=(r, q), device_id_type=MESH)

    for m in range(1, R):
        greet(lax.rem(row + m, R), c)
    for m in range(1, C):
        greet(row, lax.rem(c + m, C))
    pl.semaphore_wait(barrier, R + C - 2)

    def remote(src, dst, ssem, rsem, r, q):
        return pltpu.make_async_remote_copy(
            src_ref=src, dst_ref=dst, send_sem=ssem, recv_sem=rsem,
            device_id=(r, q), device_id_type=MESH,
        )

    mine = pl.ds(pl.multiple_of(j * chunk, chunk), chunk)

    def spread_copy(m):
        n = lax.rem(j + m, C)
        src = l_ref.at[pl.ds(pl.multiple_of(n * chunk, chunk), chunk)]
        return remote(src, mid.at[j], s0.at[m - 1], r0.at[m - 1], n * G + g, c)

    def column_copy(p, m):
        return remote(
            mid.at[p], gath.at[c, g, mine], s1.at[m - 1], r1.at[m - 1], row, p
        )

    for m in range(1, C):
        spread_copy(m).start()
    own = pltpu.make_async_copy(l_ref.at[mine], mid.at[j], own_sem.at[0])
    own.start()
    own.wait()
    for m in range(1, C):
        ref = mid.at[lax.rem(j + C - m, C)]
        remote(ref, ref, s0.at[m - 1], r0.at[m - 1], row, c).wait_recv()
    ways_on = sorted(range(1, C), key=lambda m: -min(m, C - m))
    for m in ways_on:
        column_copy(lax.rem(c + m, C), m).start()
    keep = pltpu.make_async_copy(mid.at[c], gath.at[c, g, mine], own_sem.at[1])
    keep.start()

    ta = row_tile(rows, 128)

    @pl.loop(0, rows // ta)
    def _(t):
        at = pl.ds(pl.multiple_of(t * ta, ta), ta)
        hi, lo = split(a_ref[at, :])
        a_hi[at, pl.ds(0, depth)] = hi
        a_lo[at, pl.ds(0, depth)] = lo

    order = [(0, 0), (half_ring, 0)]
    for s in range(half_ring - 1, 0, -1):
        order += [(s, -1), (s, 1)]
    blocks = []
    for s, way in order:
        blocks.append(lax.rem(c + (s if way >= 0 else C - s), C))

    def plane_copy(i, m):
        ref = gath.at[blocks[i], g, mine]
        return remote(ref, ref, s2.at[i, m - 1], r2.at[i, m - 1], lax.rem(j + m, C) * G + g, c)

    def plane_wait(i, m):
        from_j = lax.rem(j + C - m, C)
        ref = gath.at[blocks[i], g, pl.ds(pl.multiple_of(from_j * chunk, chunk), chunk)]
        remote(ref, ref, s2.at[i, m - 1], r2.at[i, m - 1], row, c).wait_recv()

    def group_copy(i, n):
        ref = gath.at[blocks[i], g]
        return remote(ref, ref, s3.at[i, n - 1], r3.at[i, n - 1], j * G + lax.rem(g + n, G), c)

    def group_wait(i, n):
        ref = gath.at[blocks[i], lax.rem(g + G - n, G)]
        remote(ref, ref, s3.at[i, n - 1], r3.at[i, n - 1], row, c).wait_recv()

    for i, (s, way) in enumerate(order):
        if s:
            m = C - s if way >= 0 else s
            ref = gath.at[blocks[i], g, mine]
            remote(ref, ref, s1.at[m - 1], r1.at[m - 1], row, c).wait_recv()
        else:
            keep.wait()
        for m in range(1, C):
            plane_copy(i, m).start()

    tb = row_tile(rows, 128)
    tm = row_tile(rows, 256)

    def multiply(i):
        q = blocks[i]
        for gg in range(G):
            @pl.loop(0, rows // tb)
            def _(t):
                hi, lo = split(gath[q, gg, pl.ds(pl.multiple_of(t * tb, tb), tb), :])
                at = pl.ds(pl.multiple_of(gg * rows + t * tb, tb), tb)
                b_hi[at, :] = hi
                b_lo[at, :] = lo

        @pl.loop(0, rows // tm)
        def _(t):
            at = pl.ds(pl.multiple_of(t * tm, tm), tm)
            dot = functools.partial(jnp.dot, preferred_element_type=jnp.float32)
            x_hi, x_lo = a_hi[at, pl.ds(0, depth)], a_lo[at, pl.ds(0, depth)]
            y_hi, y_lo = b_hi[pl.ds(0, depth), :], b_lo[pl.ds(0, depth), :]
            part[i, at, :] = dot(x_hi, y_lo) + dot(x_lo, y_hi) + dot(x_hi, y_hi)

    def ring_copy(i, way, s):
        to = lax.rem(c + (C - 1 if way == 0 else 1), C)
        piece = pl.ds(way * half, half) if s == half_ring else pl.ds(0, rows)
        return remote(
            part.at[i, piece], recv.at[way, s - 1, piece],
            s4.at[way, s - 1], r4.at[way, s - 1], row, to,
        )

    def ring_wait(way, s):
        piece = pl.ds(way * half, half) if s + 1 == half_ring else pl.ds(0, rows)
        ref = recv.at[way, s, piece]
        remote(ref, ref, s4.at[way, s], r4.at[way, s], row, c).wait_recv()

    def accumulate(i, way, s):
        lo, n = (way * half, half) if s + 1 == half_ring else (0, rows)
        step = row_tile(n, 128)

        @pl.loop(0, n // step)
        def _(t):
            at = pl.ds(pl.multiple_of(lo + t * step, 16), step)
            part[i, at, :] = part[i, at, :] + recv[way, s, at, :]

    sends = []
    for i, (s, way) in enumerate(order):
        for m in range(1, C):
            plane_wait(i, m)
        for n in range(1, G):
            group_copy(i, n).start()
        for n in range(1, G):
            group_wait(i, n)
        multiply(i)
        if s == half_ring:
            ways = (0, 1)
        elif s:
            ways = (0,) if way < 0 else (1,)
        else:
            ways = ()
        for w in ways:
            if s < half_ring:
                ring_wait(w, s)
                accumulate(i, w, s)
            copy = ring_copy(i, w, s)
            copy.start()
            sends.append(copy)

    ring_wait(0, 0)
    ring_wait(1, 0)

    @pl.loop(0, rows // ta)
    def _(t):
        at = pl.ds(pl.multiple_of(t * ta, ta), ta)
        x = part[0, at, :] + recv[0, 0, at, :] + recv[1, 0, at, :]
        out_ref[at, :] = x
        hi, lo = split(x)
        b_hi[at, :] = hi
        b_lo[at, :] = lo
        hi, lo = split(left_ref[at, :])
        a_hi[at, pl.ds(0, W)] = hi
        a_lo[at, pl.ds(0, W)] = lo

    for t in range(W // 128):
        at = pl.ds(t * 128, 128)
        dot = functools.partial(
            lax.dot_general, dimension_numbers=(((0,), (0,)), ((), ())),
            preferred_element_type=jnp.float32,
        )
        p_hi, p_lo = b_hi[pl.ds(0, rows), :], b_lo[pl.ds(0, rows), :]
        x = dot(a_hi[:, at], p_lo) + dot(a_lo[:, at], p_hi)
        gram[at, :] = x + dot(a_hi[:, at], p_hi)

    share = W // R

    def gram_copy(m):
        to = lax.rem(row + m, R)
        src = gram.at[pl.ds(pl.multiple_of(to * share, 8), share)]
        return remote(src, inbox.at[m - 1], s5.at[m - 1], r5.at[m - 1], to, c)

    for m in range(1, R):
        gram_copy(m).start()
    total = gram[pl.ds(pl.multiple_of(row * share, 8), share), :]
    for m in range(1, R):
        gram_copy(m).wait_recv()
        total = total + inbox[m - 1]
    gram_ref[...] = total

    for copy in sends:
        copy.wait_send()
    for m in range(1, C):
        spread_copy(m).wait_send()
        column_copy(lax.rem(c + m, C), m).wait_send()
    for m in range(1, R):
        gram_copy(m).wait_send()
    for i in range(C):
        for m in range(1, C):
            plane_copy(i, m).wait_send()
        for n in range(1, G):
            group_copy(i, n).wait_send()


def grid_product(R, C, a, l, left):
    rows, cols = l.shape
    G = R // C
    depth = a.shape[1]
    vmem = pl.BlockSpec(memory_space=pltpu.VMEM)
    dma = pltpu.SemaphoreType.DMA
    return pl.pallas_call(
        functools.partial(product_kernel, R, C),
        out_shape=[
            jax.ShapeDtypeStruct((rows, cols), jnp.float32),
            jax.ShapeDtypeStruct((W // R, cols), jnp.float32),
        ],
        in_specs=[vmem, vmem, vmem],
        out_specs=[vmem, vmem],
        scratch_shapes=[
            pltpu.VMEM((C, rows // C, cols), jnp.float32),
            pltpu.VMEM((C, G, rows, cols), jnp.float32),
            pltpu.VMEM((C, rows, cols), jnp.float32),
            pltpu.VMEM((2, C // 2, rows, cols), jnp.float32),
            pltpu.VMEM((W, cols), jnp.float32),
            pltpu.VMEM((R - 1, W // R, cols), jnp.float32),
            pltpu.VMEM((rows, max(depth, W)), jnp.bfloat16),
            pltpu.VMEM((rows, max(depth, W)), jnp.bfloat16),
            pltpu.VMEM((max(depth, rows), cols), jnp.bfloat16),
            pltpu.VMEM((max(depth, rows), cols), jnp.bfloat16),
            dma((C - 1,)),
            dma((C - 1,)),
            dma((C - 1,)),
            dma((C - 1,)),
            dma((C, C - 1)),
            dma((C, C - 1)),
            dma((C, max(G - 1, 1))),
            dma((C, max(G - 1, 1))),
            dma((2, C // 2)),
            dma((2, C // 2)),
            dma((R - 1,)),
            dma((R - 1,)),
            dma((2,)),
        ],
        compiler_params=pltpu.CompilerParams(
            collective_id=0, has_side_effects=True, vmem_limit_bytes=67043328
        ),
    )(a, l, left)


CUTS = 2


def pieces_of(tiles):
    sizes = [1]
    while sum(sizes) < tiles:
        sizes.append(2 if tiles - sum(sizes) > 2 else 1)
    return [(sum(sizes[:p]), n) for p, n in enumerate(sizes)]


def line_kernel(
    R, C, a_hbm, f_hbm, diag_ref, widths_ref, member_ref, out_ref, dout_ref,
    a_raw, mask, lm, mid, gath, part, recv, a_hi, a_lo, b_hi, b_lo, t_hi, t_lo,
    gram, pair, inbox, in_sem, own_sem, s0, r0, s1, r1, s2, r2, s3, r3, s4, r4, s5, r5, s6, r6, s7, r7,
):
    rows, depth = a_raw.shape
    tiles = lm.shape[0]
    G = R // C
    chunk = rows // C
    half = chunk // 2
    share = W // R
    pieces = pieces_of(tiles)
    row = lax.axis_index("row")
    c = lax.axis_index("col")
    j = row // G
    g = lax.rem(row, G)
    other = 1 - g
    jx = j + 1 - 2 * lax.rem(j, 2)
    jy = lax.rem(j + 2, C)
    jd = C - 1 - j
    last = C - 1
    h = c // 2
    m = c + h * (last - 2 * c)

    def flip(n):
        return n + h * (last - 2 * n)

    blocks = [flip(3), flip(2 - 2 * m), flip(1 + m), c]
    onward = [flip(m + 1), flip(1 - m), flip(m + 1)]
    slots = [blocks[0], blocks[1], blocks[2] + m * (C - blocks[2])]

    def load_f(t):
        return pltpu.make_async_copy(f_hbm.at[:, pl.ds(t * 128, 128)], lm.at[t], in_sem.at[t])

    load_a = pltpu.make_async_copy(a_hbm, a_raw, in_sem.at[tiles])
    for t in range(tiles):
        load_f(t).start()
    load_a.start()

    barrier = pltpu.get_barrier_semaphore()

    def greet(r, q):
        pl.semaphore_signal(barrier, inc=1, device_id=(r, q), device_id_type=MESH)

    for n in range(1, R):
        greet(lax.rem(row + n, R), c)

    for n in range(1, C):
        greet(row, lax.rem(c + n, C))

    keep = lax.broadcasted_iota(jnp.int32, (NODES, 128), 0) == c
    width = widths_ref[c]
    member = member_ref[...].astype(jnp.float32).astype(jnp.bfloat16)

    def make_mask(t):
        q = lax.broadcasted_iota(jnp.int32, (NODES, 128), 1) + t * 128
        pick = jnp.where(keep & (q < width), 1.0, 0.0).astype(jnp.bfloat16)
        x = lax.dot_general(
            member, pick, (((0,), (0,)), ((), ())), preferred_element_type=jnp.float32
        )
        load_f(t).wait()
        mask[t] = x
        lm[t] = lm[t] * x

    for t in range(pieces[0][1]):
        make_mask(t)

    pl.semaphore_wait(barrier, R + C - 2)

    def remote(src, dst, ssem, rsem, r, q):
        return pltpu.make_async_remote_copy(
            src_ref=src, dst_ref=dst, send_sem=ssem, recv_sem=rsem,
            device_id=(r, q), device_id_type=MESH,
        )

    def at_tiles(p):
        t, n = pieces[p]
        return pl.ds(t, n)

    def spot(gg, jj, n=None, k=0):
        start = gg * rows + jj * chunk + k * half
        return pl.ds(pl.multiple_of(start, 8), half if n else chunk)

    mine = pl.ds(pl.multiple_of(j * chunk, 8), chunk)
    near = [j, jx, jy, jd]

    def spread_copy(d, p):
        src = lm.at[at_tiles(p), pl.ds(pl.multiple_of(near[d] * chunk, 8), chunk)]
        dst = mid.at[d - 1, at_tiles(p)]
        return remote(src, dst, s0.at[d - 1, p], r0.at[d - 1, p], near[d] * G + g, c)

    def spread_start(p, ways=(1, 2, 3)):
        for d in ways:
            spread_copy(d, p).start()

    def line_source(d, p):
        return mid.at[d - 1, at_tiles(p)] if d else lm.at[at_tiles(p), mine]

    def line_copy(d, p):
        dst = gath.at[c, at_tiles(p), spot(g, j)]
        return remote(line_source(d, p), dst, s6.at[d, p], r6.at[c, p], row, near[d])

    def keep_copy(d, p):
        dst = gath.at[c, at_tiles(p), spot(g, j)]
        return pltpu.make_async_copy(line_source(d, p), dst, own_sem.at[p])

    def line_start(d, p):
        if d:
            spread_copy(d, p).wait_recv()

        @pl.when(near[d] != c)
        def _():
            line_copy(d, p).start()

        @pl.when(near[d] == c)
        def _():
            keep_copy(d, p).start()

    def line_sent(p):
        for d in range(C):
            @pl.when(near[d] != c)
            def _():
                line_copy(d, p).wait_send()

    spread_start(0, (1, 2, 3))
    line_start(0, 0)
    for t in range(pieces[0][1], tiles):
        make_mask(t)
    spread_start(1, (1, 2, 3))
    for d in range(1, C):
        line_start(d, 0)
    for p in range(2, len(pieces)):
        spread_start(p)
    for p in range(1, len(pieces)):
        line_start(0, p)
    load_a.wait()
    ta = row_tile(rows, 128)

    @pl.loop(0, rows // ta)
    def _(t):
        at = pl.ds(pl.multiple_of(t * ta, ta), ta)
        hi, lo = split(a_raw[at, :])
        a_hi[at, :] = hi
        a_lo[at, :] = lo

    for t in range(tiles):
        hi, lo = split(lm[t].T)
        t_hi[pl.ds(t * 128, 128), :] = hi
        t_lo[pl.ds(t * 128, 128), :] = lo

    for p in range(1, len(pieces)):
        for d in range(1, C):
            line_start(d, p)
    units = [(i, p) for p in range(len(pieces)) for i in range(C)]

    def take(u):
        i, p = units[u]
        if i == C - 1:
            keep_copy(0, p).wait()
        else:
            ref = gath.at[blocks[i], at_tiles(p), spot(g, j)]
            remote(ref, ref, s6.at[0, p], r6.at[blocks[i], p], row, c).wait_recv()

    def pass_copy(u, way):
        i, p = units[u]
        ref = gath.at[blocks[i], at_tiles(p), spot(g, j)]
        to = jx if way == 0 else jy
        return remote(ref, ref, s1.at[u, way], r1.at[u, way], to * G + g, c)

    def pass_wait(u, way):
        i, p = units[u]
        ref = gath.at[blocks[i], at_tiles(p), spot(g, jx if way == 0 else jy)]
        remote(ref, ref, s1.at[u, way], r1.at[u, way], row, c).wait_recv()

    def forward_copy(u, way):
        i, p = units[u]
        ref = gath.at[blocks[i], at_tiles(p), spot(g, jx if way == 0 else jy, 1, way)]
        to = jy if way == 0 else jx
        return remote(ref, ref, s2.at[u, way], r2.at[u, way], to * G + g, c)

    def forward_wait(u, way):
        i, p = units[u]
        ref = gath.at[blocks[i], at_tiles(p), spot(g, jd, 1, way)]
        remote(ref, ref, s2.at[u, way], r2.at[u, way], row, c).wait_recv()

    def swap_copy(u):
        i, p = units[u]
        ref = gath.at[blocks[i], at_tiles(p), pl.ds(pl.multiple_of(g * rows, 8), rows)]
        return remote(ref, ref, s3.at[u], r3.at[u], j * G + other, c)

    def swap_wait(u):
        i, p = units[u]
        ref = gath.at[blocks[i], at_tiles(p), pl.ds(pl.multiple_of(other * rows, 8), rows)]
        remote(ref, ref, s3.at[u], r3.at[u], row, c).wait_recv()

    def bands(p):
        n = CUTS if p == len(pieces) - 1 else 1
        return [(p + k, k * (rows // n), rows // n) for k in range(n)]

    def sum_copy(u, band):
        i, p = units[u]
        sem, lo, n = band
        at = pl.ds(lo, n)
        return remote(
            part.at[i, at_tiles(p), at], recv.at[slots[i], at_tiles(p), at],
            s4.at[i, sem], r4.at[slots[i], sem], row, onward[i],
        )

    def sum_sent(u):
        for band in bands(units[u][1]):
            sum_copy(u, band).wait_send()

    def sum_wait(slot, p, band):
        sem, lo, n = band
        ref = recv.at[slot, at_tiles(p), pl.ds(lo, n)]
        remote(ref, ref, s4.at[0, sem], r4.at[slot, sem], row, c).wait_recv()

    def stage_a(u):
        take(u)
        for way in range(2):
            pass_copy(u, way).start()

    def stage_b(u):
        for way in range(2):
            pass_wait(u, way)
            forward_copy(u, way).start()

    def stage_c(u):
        for way in range(2):
            forward_wait(u, way)
        swap_copy(u).start()

    tb = row_tile(depth, 256)
    tm = row_tile(rows, 384)

    def stage_d(u):
        i, p = units[u]
        t0, n = pieces[p]
        q = blocks[i]
        cols = pl.ds(0, n * 128)
        swap_wait(u)

        @pl.loop(0, depth // tb)
        def _(t):
            at = pl.ds(pl.multiple_of(t * tb, tb), tb)
            for k in range(n):
                hi, lo = split(gath[q, t0 + k, at, :])
                b_hi[at, pl.ds(k * 128, 128)] = hi
                b_lo[at, pl.ds(k * 128, 128)] = lo

        @pl.loop(0, rows // tm)
        def _(t):
            at = pl.ds(pl.multiple_of(t * tm, tm), tm)
            dot = functools.partial(jnp.dot, preferred_element_type=jnp.float32)
            x = dot(a_hi[at, :], b_lo[:, cols]) + dot(a_lo[at, :], b_hi[:, cols])
            x = x + dot(a_hi[at, :], b_hi[:, cols])
            for k in range(n):
                part[i, t0 + k, at, :] = x[:, k * 128:(k + 1) * 128]

        if i < C - 1:
            @pl.when(m == 0)
            def _():
                for k, band in enumerate(bands(p)):
                    ahead = in_flight + [(u, b) for b in bands(p)[:k]]
                    if len(ahead) > 1:
                        sum_copy(*ahead[-2]).wait_send()
                    sum_copy(u, band).start()

            in_flight.extend((u, band) for band in bands(p))

    def add_in(i, slot, p, band):
        t0, n = pieces[p]
        sem, lo, many = band
        step = row_tile(many, 128)

        @pl.loop(0, many // step)
        def _(t):
            at = pl.ds(pl.multiple_of(lo + t * step, 16), step)
            for k in range(n):
                part[i, t0 + k, at, :] = part[i, t0 + k, at, :] + recv[slot, t0 + k, at, :]

    def stage_e(u):
        i, p = units[u]

        @pl.when(m == 1)
        def _():
            for band in bands(p):
                sum_wait(blocks[i], p, band)
                add_in(i, blocks[i], p, band)
                sum_copy(u, band).start()

    def pair_copy(p):
        return remote(
            gram.at[at_tiles(p), other], pair.at[at_tiles(p)],
            s7.at[p], r7.at[p], j * G + other, c,
        )

    def gram_copy(d, p):
        return remote(
            gram.at[at_tiles(p), g, near[d]], inbox.at[d - 1, at_tiles(p)],
            s5.at[d - 1, p], r5.at[d - 1, p], near[d] * G + g, c,
        )

    def stage_p(p):
        t0, n = pieces[p]
        pair_copy(p).wait_recv()
        for k in range(n):
            gram[t0 + k, g] = gram[t0 + k, g] + pair[t0 + k]
        for d in range(C - 1, 0, -1):
            gram_copy(d, p).start()

    def stage_f(p):
        t0, n = pieces[p]
        cols = pl.ds(0, n * 128)

        @pl.when(m == 1)
        def _():
            for band in bands(p):
                sum_wait(C, p, band)
                add_in(C - 1, C, p, band)

        def finish(band):
            sum_wait(c, p, band)
            sem, lo, many = band
            step = row_tile(many, 128)

            @pl.loop(0, many // step)
            def _(t):
                at = pl.ds(pl.multiple_of(lo + t * step, 16), step)
                for k in range(n):
                    x = part[C - 1, t0 + k, at, :] + recv[c, t0 + k, at, :]
                    out_ref[at, pl.ds((t0 + k) * 128, 128)] = -x * mask[t0 + k, at, :]
                    hi, lo_part = split(x)
                    b_hi[at, pl.ds(k * 128, 128)] = hi
                    b_lo[at, pl.ds(k * 128, 128)] = lo_part

        for band in bands(p):
            finish(band)

        dot = functools.partial(jnp.dot, preferred_element_type=jnp.float32)
        p_hi, p_lo = b_hi[pl.ds(0, rows), cols], b_lo[pl.ds(0, rows), cols]
        for r in range(0, R, 4):
            at = pl.ds(r * share, 4 * share)
            x = dot(t_hi[at, :], p_lo) + dot(t_lo[at, :], p_hi) + dot(t_hi[at, :], p_hi)
            for e in range(4):
                for k in range(n):
                    y = x[e * share:(e + 1) * share, k * 128:(k + 1) * 128]
                    gram[t0 + k, (r + e) % G, (r + e) // G] = y
        pair_copy(p).start()

    def stage_g(p):
        t0, n = pieces[p]
        for d in range(1, C):
            gram_copy(d, p).wait_recv()
        for k in range(n):
            t = t0 + k
            x = gram[t, g, j]
            for d in range(C - 1):
                x = x + inbox[d, t]
            at = pl.ds(t * 128, 128)
            r = lax.broadcasted_iota(jnp.int32, (share, 128), 0) + row * share
            q = lax.broadcasted_iota(jnp.int32, (share, 128), 1) + t * 128
            inside = (r < width) & (q < width)
            dout_ref[:, at] = jnp.where(inside, diag_ref[:, at] + x, 0.0)

    total = len(units)
    finished = 0
    in_flight = []

    def due(u, lag):
        wait = 1 if u >= C else 0
        return u + lag + wait

    for step in range(due(total, 7)):
        for u in range(total):
            i, p = units[u]
            if due(u, 7) == step:
                if i < C - 1:
                    stage_e(u)
                if p and i == (0 if p == len(pieces) - 1 else C - 2):
                    if p > 1:
                        stage_p(p - 2)
                    stage_f(p - 1)
                    finished = p
        for lag, stage in ((3, stage_d), (2, stage_c), (1, stage_b), (0, stage_a)):
            for u in range(total):
                if due(u, lag) == step:
                    stage(u)
    for p in range(finished, len(pieces)):
        if p > 0:
            stage_p(p - 1)
        stage_f(p)
    stage_p(len(pieces) - 1)
    for p in range(len(pieces)):
        stage_g(p)

    for p in range(len(pieces)):
        line_sent(p)
        for d in range(1, C):
            spread_copy(d, p).wait_send()
        for d in range(1, C):
            gram_copy(d, p).wait_send()
        pair_copy(p).wait_send()
    for u in range(total):
        for way in range(2):
            pass_copy(u, way).wait_send()
            forward_copy(u, way).wait_send()
        swap_copy(u).wait_send()

    @pl.when(m == 0)
    def _():
        for u, band in in_flight[-2:]:
            sum_copy(u, band).wait_send()

    @pl.when(m == 1)
    def _():
        for u in range(total):
            if units[u][0] < C - 1:
                sum_sent(u)


def line_product(R, C, a, f, diag, widths, member):
    rows, depth = a.shape
    cols = f.shape[1]
    tiles = cols // 128
    pieces = len(pieces_of(tiles))
    units = C * pieces
    f32, bf16 = jnp.float32, jnp.bfloat16
    vmem = pl.BlockSpec(memory_space=pltpu.VMEM)
    smem = pl.BlockSpec(memory_space=pltpu.SMEM)
    hbm = pl.BlockSpec(memory_space=pl.ANY)
    dma = pltpu.SemaphoreType.DMA
    return pl.pallas_call(
        functools.partial(line_kernel, R, C),
        out_shape=[
            pltpu.VMEM((rows, cols), f32),
            pltpu.VMEM((W // R, cols), f32),
        ],
        in_specs=[hbm, hbm, vmem, smem, vmem],
        out_specs=[vmem, vmem],
        scratch_shapes=[
            pltpu.VMEM((rows, depth), f32),
            pltpu.VMEM((tiles, rows, 128), f32),
            pltpu.VMEM((tiles, rows, 128), f32),
            pltpu.VMEM((C - 1, tiles, rows // C, 128), f32),
            pltpu.VMEM((C, tiles, depth, 128), f32),
            pltpu.VMEM((C, tiles, rows, 128), f32),
            pltpu.VMEM((C + 1, tiles, rows, 128), f32),
            pltpu.VMEM((rows, depth), bf16),
            pltpu.VMEM((rows, depth), bf16),
            pltpu.VMEM((depth, 256), bf16),
            pltpu.VMEM((depth, 256), bf16),
            pltpu.VMEM((W, rows), bf16),
            pltpu.VMEM((W, rows), bf16),
            pltpu.VMEM((tiles, R // C, C, W // R, 128), f32),
            pltpu.VMEM((tiles, C, W // R, 128), f32),
            pltpu.VMEM((C - 1, tiles, W // R, 128), f32),
            dma((tiles + 1,)),
            dma((pieces,)),
            dma((C - 1, pieces)),
            dma((C - 1, pieces)),
            dma((units, 2)),
            dma((units, 2)),
            dma((units, 2)),
            dma((units, 2)),
            dma((units,)),
            dma((units,)),
            dma((C - 1, pieces + CUTS - 1)),
            dma((C + 1, pieces + CUTS - 1)),
            dma((C - 1, pieces)),
            dma((C - 1, pieces)),
            dma((C, pieces)),
            dma((C, pieces)),
            dma((pieces,)),
            dma((pieces,)),
        ],
        compiler_params=pltpu.CompilerParams(
            collective_id=1, has_side_effects=True, vmem_limit_bytes=64000000
        ),
    )(a, f, diag, widths, member)


def per_device(ancestor_inverse, factor, diag_inverse, widths, member):
    R = lax.axis_size("row")
    C = lax.axis_size("col")
    my_row = lax.axis_index("row")
    my_col = lax.axis_index("col")
    shard_cols = factor.shape[1]
    rows, depth = ancestor_inverse.shape
    if C == NODES and R == 2 * C and shard_cols == W and depth == 2 * rows:
        return tuple(line_product(R, C, ancestor_inverse, factor, diag_inverse, widths, member))
    col_start = my_col * shard_cols
    global_cols = col_start + jnp.arange(shard_cols, dtype=jnp.int32)
    node_of = global_cols // W
    within = global_cols % W
    select = node_of[None, :] == jnp.arange(NODES, dtype=jnp.int32)[:, None]
    width_col = jnp.sum(jnp.where(select, widths[:, None], 0), axis=0)
    col_keep = within < width_col
    pick = jnp.where(select & col_keep[None, :], 1.0, 0.0).astype(jnp.bfloat16)
    mask = lax.dot_general(
        member.astype(jnp.bfloat16), pick, (((0,), (0,)), ((), ())),
        preferred_element_type=jnp.float32,
    )
    masked = factor * mask
    if shard_cols == W:
        left = masked
    else:
        rows_full = lax.all_gather(masked, "col", axis=1, tiled=True)
        left = lax.dynamic_slice_in_dim(rows_full, col_start // W * W, W, 1)
    product, gram = grid_product(R, C, ancestor_inverse, masked, left)
    offdiag = -product * mask
    diag_rows = diag_inverse.shape[0]
    local_rows = my_row * diag_rows + jnp.arange(diag_rows, dtype=jnp.int32)
    inside = (local_rows[:, None] < width_col[None, :]) & col_keep[None, :]
    diag_blocks = (diag_inverse + gram) * inside.astype(jnp.float32)
    return (offdiag, diag_blocks)


def solution(mesh):
    in_specs = (P("row", "col"), P("row", "col"), P("row", "col"), P(), P(None, "row"))
    out_specs = (P("row", "col"), P("row", "col"))
    return jax.shard_map(
        per_device, mesh=mesh, in_specs=in_specs, out_specs=out_specs, check_vma=False
    )
```
